32 devices in a mesh: row: 8 (over z, x), ch: 4 (over y, core).
Axes of the slice: x: 2, y: 2, z: 4, core: 2. Of those that a mesh axis runs over, the one named last changes fastest.
Arguments:
- pair_rep: bfloat16 [128, 8, 8], P('ch', 'row'), may hold values from -6 to 6
- residue_mask: int32 [8], replicated, may hold values 0 or 1
- chain_ids: int32 [8], replicated, may hold values from 0 to 3, never falling along the last dimension, each value on 1 to 4 neighbouring positions
- in_gain: float32 [2, 128], replicated, may hold values from 0.5 to 1.5
- in_bias: float32 [2, 128], replicated, may hold values from -3 to 3
- w_proj: bfloat16 [2, 128, 4, 128], P(None, None, None, 'ch'), may hold values from -0.5 to 0.5
- w_gate: bfloat16 [2, 128, 128], P(None, None, 'ch'), may hold values from -0.5 to 0.5
- pair_bias: float32 [2, 128], P(None, 'ch'), may hold values from -4 to 4
- out_gain: float32 [2, 128], P(None, 'ch'), may hold values from 0.5 to 1.5
- out_bias: float32 [2, 128], P(None, 'ch'), may hold values from -3 to 3
- w_out: bfloat16 [2, 128, 128], P(None, 'ch'), may hold values from -0.5 to 0.5
Outputs:
- pair_out: bfloat16 [128, 8, 8], P('ch', 'row')
The draws below stay inside these ranges and needn't reach their ends.
Inputs may be any that keep to these rules, and one draw needn't show every extreme that they name: `chain_ids`: chain numbers never fall along the residues; each chain has 1 to 4 residues.
All inputs are finite; a program needn't handle non-finite values.
Results may differ from the reference program's by a relative error of at most 0.013.
Values may be sent and summed in bfloat16 or wider, within the bound.
A program may use at most 64 MiB of HBM per device.

```python
import math
import jax
import jax.numpy as jnp
import numpy as np
from jax import lax

C = 128
CH = 128
N = 8


def place_ends(array, own_key, least, largest):
    longest = array.shape.index(max(array.shape))
    spots = []
    for shift in (0, 1):
        where = [jax.random.randint(jax.random.fold_in(own_key, axis), (), 0, length) for axis, length in enumerate(array.shape)]
        where[longest] = (where[longest] + shift) % array.shape[longest]
        spots.append(tuple(where))
    return array.at[spots[0]].set(least).at[spots[1]].set(largest)


def shard_levels(key, shape, cuts, smallest, largest):
    level = 1.0
    for position, shards_of in cuts:
        draws = jax.random.uniform(jax.random.fold_in(jax.random.fold_in(key, 6), position), (shards_of,), jnp.float32, smallest / len(cuts), largest / len(cuts))
        level = level * jnp.repeat(jnp.exp(draws), shape[position] // shards_of).reshape((-1,) + (1,) * (len(shape) - 1 - position))
    return level


def split_up(amount, total, reach, lean):
    weights = [(1 << 20) // math.isqrt(grade ** lean) + 1 for grade in range(2, amount + 1)]
    spare, counts = total - reach - (amount - 1), [1] * (amount - 1)
    while spare > 0:
        movable = [i for i in range(amount - 1) if counts[i] < reach]
        whole, left = sum([weights[i] for i in movable]), spare
        for i in movable:
            addition = min(reach - counts[i], max(1, left * weights[i] // whole), spare)
            counts[i] = counts[i] + addition
            spare = spare - addition
    return np.array([reach] + counts)


def uneven(rng, amount, total, bound, skew):
    if amount == 2:
        one = jax.random.randint(rng, (), max(1, total - bound), min(bound, total - 1) + 1)
        return jnp.stack([one, total - one])
    lengths = jnp.asarray(split_up(amount, total, bound, skew), jnp.int32)
    twos = (amount - 1) // 2
    source_of, receiver = lengths[1:1 + 2 * twos:2], lengths[2:2 + 2 * twos:2]
    slack = jnp.minimum(source_of - 1, bound - receiver)
    passed = jax.random.randint(jax.random.fold_in(rng, 1), (twos,), 0, 1 << 20) % (slack + 1)
    lengths = lengths.at[1:1 + 2 * twos:2].set(source_of - passed).at[2:2 + 2 * twos:2].set(receiver + passed)
    return lengths[jax.random.permutation(jax.random.fold_in(rng, 2), amount)]


def bell_draw(own_key, shape, scale, bound, split=(), held_as=jnp.bfloat16):
    drawn = scale * jax.random.normal(own_key, shape, jnp.float32)
    if split:
        drawn = drawn * shard_levels(own_key, shape, split, -0.22, 0.18)
    return jnp.clip(drawn, -bound, bound).astype(held_as)


def setup_inputs(seed: int = 0) -> dict:
    arg_keys = jax.random.split(jax.random.key(seed), 12)
    return {
        "pair_rep": bell_draw(arg_keys[0], (C, N, N), 1.0, 6.0, ((0, 4), (1, 8))),
        "residue_mask": place_ends((jax.random.randint(arg_keys[1], (N,), 0, 8) < 7).astype(jnp.int32), jax.random.fold_in(arg_keys[1], 1), 0, 1),
        "chain_ids": jnp.searchsorted(jnp.cumsum(uneven(arg_keys[2], 4, N, N // 2, 1)), jnp.arange(N), side="right").astype(jnp.int32),
        "in_gain": jnp.clip(1.0 + 0.1 * jax.random.normal(arg_keys[3], (2, C), jnp.float32), 0.5, 1.5),
        "in_bias": bell_draw(arg_keys[4], (2, C), 0.5, 3.0, (), jnp.float32),
        "w_proj": bell_draw(arg_keys[5], (2, C, 4, CH), C ** -0.5, 0.5, ((3, 4),)),
        "w_gate": bell_draw(arg_keys[6], (2, C, C), C ** -0.5, 0.5, ((2, 4),)),
        "pair_bias": bell_draw(arg_keys[7], (2, C), 1.0, 4.0, ((1, 4),), jnp.float32),
        "out_gain": jnp.clip(1.0 + 0.1 * jax.random.normal(arg_keys[8], (2, CH), jnp.float32), 0.5, 1.5),
        "out_bias": bell_draw(arg_keys[9], (2, CH), 0.5, 3.0, ((1, 4),), jnp.float32),
        "w_out": bell_draw(arg_keys[10], (2, CH, C), CH ** -0.5, 0.5, ((1, 4),)),
    }


epsilon = 1e-05

def channel_norm(values, norm_gain, norm_bias):
    mean_val = lax.optimization_barrier(jnp.mean(values, axis=0))
    variance = lax.optimization_barrier(jnp.mean(values * values, axis=0)) - mean_val * mean_val
    return (values - mean_val) * lax.rsqrt(variance + epsilon) * norm_gain[:, None, None] + norm_bias[:, None, None]

def reference(pair_rep, residue_mask, chain_ids, in_gain, in_bias, w_proj, w_gate, pair_bias, out_gain, out_bias, w_out):
    mask_float = residue_mask.astype(jnp.float32)
    pair_mask = mask_float[:, None] * mask_float[None, :]
    same_chain = (chain_ids[:, None] == chain_ids[None, :]).astype(jnp.float32)

    def update(pair_in, layer, incoming):
        normed = channel_norm(pair_in.astype(jnp.float32), in_gain[layer], in_bias[layer]).astype(jnp.bfloat16)
        normed_f = normed.astype(jnp.float32)
        projected = jnp.einsum('cij,cpd->pdij', normed_f, w_proj[layer].astype(jnp.float32))
        left_arm = (jax.nn.sigmoid(projected[0]) * projected[1] * pair_mask).astype(jnp.bfloat16).astype(jnp.float32)
        right_arm = (jax.nn.sigmoid(projected[2]) * projected[3] * pair_mask).astype(jnp.bfloat16).astype(jnp.float32)
        if incoming:
            product_sum = jnp.einsum('dki,dkj->dij', left_arm, right_arm)
        else:
            product_sum = jnp.einsum('dik,djk->dij', left_arm, right_arm)
        normed_x = channel_norm(product_sum, out_gain[layer], out_bias[layer]).astype(jnp.bfloat16)
        mixed = jnp.einsum('dij,dc->cij', normed_x.astype(jnp.float32), w_out[layer].astype(jnp.float32))
        logits = jnp.einsum('cij,cd->dij', normed_f, w_gate[layer].astype(jnp.float32)) + pair_bias[layer][:, None, None] * same_chain[None]
        return (pair_in.astype(jnp.float32) + jax.nn.sigmoid(logits) * mixed).astype(jnp.bfloat16)
    middle = update(pair_rep, 0, False)
    return update(middle, 1, True)
```

```python
import functools
import jax
import jax.numpy as jnp
from jax import lax
from jax.experimental import pallas as pl
from jax.experimental.pallas import tpu as pltpu
from jax.sharding import PartitionSpec as P

epsilon = 1e-05
MESH = pl.DeviceIdType.MESH
F32 = jnp.float32
BF16 = jnp.bfloat16


def lane_norm(values, gain, bias):
    mean_val = jnp.mean(values, axis=-1, keepdims=True)
    variance = jnp.mean(values * values, axis=-1, keepdims=True) - mean_val * mean_val
    return ((values - mean_val) * lax.rsqrt(variance + epsilon) * gain + bias).astype(BF16)


def dot_nt(a, b):
    return lax.dot_general(a, b, (((1,), (1,)), ((), ())), preferred_element_type=F32)


def dot_nn(a, b):
    return lax.dot_general(a, b, (((1,), (0,)), ((), ())), preferred_element_type=F32)


def drain(ref, sem):
    pltpu.make_async_copy(ref, ref, sem).wait()


def window_kernel(
    rows,
    chs,
    mask_hbm,
    chain_hbm,
    pair_hbm,
    in_gain_hbm,
    in_bias_hbm,
    proj_hbm,
    gate_hbm,
    bias_hbm,
    gain_hbm,
    offset_hbm,
    mix_hbm,
    out_ref,
    mask_ref,
    chain_ref,
    norm_buf,
    block_buf,
    proj_buf,
    gate_buf,
    mix_buf,
    vector_buf,
    left_buf,
    right_buf,
    middle_buf,
    normed_buf,
    ready_sem,
    scalar_sem,
    norm_sem,
    block_send,
    block_recv,
    vector_send,
    vector_recv,
    weight_send,
    weight_recv,
):
    n = out_ref.shape[0]
    lanes = norm_buf.shape[2]
    block = lanes // chs
    row = lax.axis_index("row")
    ch = lax.axis_index("ch")
    peers = [lax.rem(ch + step, chs) for step in range(1, chs)]

    barrier = pltpu.get_barrier_semaphore()
    for peer in peers:
        pl.semaphore_signal(barrier, inc=1, device_id=(row, peer), device_id_type=MESH)

    @pl.loop(row + 1, rows)
    def _(other):
        for m in range(chs):
            pl.semaphore_signal(barrier, inc=1, device_id=(other, m), device_id_type=MESH)

    pltpu.make_async_copy(mask_hbm, mask_ref, scalar_sem.at[0]).start()
    pltpu.make_async_copy(chain_hbm, chain_ref, scalar_sem.at[1]).start()
    pltpu.make_async_copy(in_gain_hbm, norm_buf.at[0], norm_sem.at[0]).start()
    pltpu.make_async_copy(in_bias_hbm, norm_buf.at[1], norm_sem.at[1]).start()
    here = row * chs + ch
    pltpu.make_async_copy(pair_hbm, block_buf.at[here], block_recv).start()
    vectors = [
        (ref, vector_buf.at[t, ch], vector_send.at[t], vector_recv.at[t])
        for t, ref in enumerate((bias_hbm, gain_hbm, offset_hbm))
    ]
    weights = [
        [
            (ref.at[u], buf.at[u, ch], weight_send.at[u, t], weight_recv.at[u, t])
            for t, (ref, buf) in enumerate(
                ((proj_hbm, proj_buf), (gate_hbm, gate_buf), (mix_hbm, mix_buf))
            )
        ]
        for u in range(2)
    ]
    for src, dst, _, recv in weights[0] + vectors + weights[1]:
        pltpu.make_async_copy(src, dst, recv).start()

    def send(src, dst, send_sem, recv_sem, r, c):
        pltpu.make_async_remote_copy(
            src_ref=src,
            dst_ref=dst,
            send_sem=send_sem,
            recv_sem=recv_sem,
            device_id=(r, c),
            device_id_type=MESH,
        ).start()

    def send_block(r, c):
        send(pair_hbm, block_buf.at[here], block_send, block_recv, r, c)

    pl.semaphore_wait(barrier, chs - 1 + row * chs)

    @pl.loop(0, row)
    def _(other):
        for m in range(chs):
            send_block(other, m)
            pl.semaphore_signal(
                ready_sem.at[row], inc=1, device_id=(other, m), device_id_type=MESH
            )

    for peer in peers:
        send_block(row, peer)
    for src, dst, send_sem, recv_sem in weights[0] + vectors + weights[1]:
        for peer in peers:
            send(src, dst, send_sem, recv_sem, row, peer)

    @pl.loop(row + 1, rows)
    def _(other):
        pl.semaphore_wait(ready_sem.at[other], chs)
        for m in range(chs):
            send_block(other, m)

    drain(mask_hbm, scalar_sem.at[0])
    drain(chain_hbm, scalar_sem.at[1])
    place = lax.broadcasted_iota(jnp.int32, (n, lanes), 0)
    mask_j = jnp.zeros((n, lanes), jnp.int32)
    chain_j = jnp.zeros((n, lanes), jnp.int32)
    for j in range(n):
        mask_j = jnp.where(place == j, mask_ref[j], mask_j)
        chain_j = jnp.where(place == j, chain_ref[j], chain_j)
    pair_mask = jnp.concatenate([(mask_j * mask_ref[i]).astype(F32) for i in range(n)], axis=0)
    same_chain = jnp.concatenate(
        [jnp.where(chain_j == chain_ref[i], 1.0, 0.0).astype(F32) for i in range(n)], axis=0
    )
    same_here = jnp.where(chain_j == chain_ref[row], 1.0, 0.0).astype(F32)

    def projection(u, part):
        part_rows = slice(part * block, (part + 1) * block)
        return proj_buf[u, :, part_rows, :].reshape(lanes, lanes)

    def vector(t, u):
        return jnp.concatenate([vector_buf[t, m, u : u + 1, :] for m in range(chs)], axis=1)

    def arms(u, normed):
        left = jax.nn.sigmoid(dot_nt(normed, projection(u, 0))) * dot_nt(normed, projection(u, 1))
        right = jax.nn.sigmoid(dot_nt(normed, projection(u, 2))) * dot_nt(normed, projection(u, 3))
        left_buf[...] = (left * pair_mask).astype(BF16).astype(F32)
        right_buf[...] = (right * pair_mask).astype(BF16).astype(F32)

    def update(u, pair, normed, product, same):
        xn = lane_norm(product, vector(1, u), vector(2, u))
        mixed = dot_nn(xn, mix_buf[u].reshape(lanes, lanes))
        logits = dot_nt(normed, gate_buf[u].reshape(lanes, lanes)) + vector(0, u) * same
        return (pair + jax.nn.sigmoid(logits) * mixed).astype(BF16)

    def normalize(u, pair):
        return lane_norm(pair, norm_buf[0, u : u + 1, :], norm_buf[1, u : u + 1, :])

    def arrive(u):
        for t, buf in enumerate((proj_buf, gate_buf, mix_buf)):
            drain(buf.at[u], weight_recv.at[u, t])

    drain(norm_buf.at[0], norm_sem.at[0])
    drain(norm_buf.at[1], norm_sem.at[1])
    for t in range(3):
        drain(vector_buf.at[t], vector_recv.at[t])
    arrive(0)
    drain(block_buf, block_recv)
    pair = jnp.concatenate(
        [
            jnp.concatenate([block_buf[i * chs + m].astype(F32) for m in range(chs)], axis=1)
            for i in range(n)
        ],
        axis=0,
    )
    normed = normalize(0, pair)
    arms(0, normed)
    right_k = [right_buf[pl.ds(k, n, stride=n), :] for k in range(n)]
    product = []
    for i in range(n):
        total = left_buf[i * n : i * n + 1, :] * right_k[0]
        for k in range(1, n):
            total = total + left_buf[i * n + k : i * n + k + 1, :] * right_k[k]
        product.append(total)
    middle = update(0, pair, normed, jnp.concatenate(product, axis=0), same_chain).astype(F32)
    middle_buf[...] = middle

    normed = normalize(1, middle)
    normed_buf[...] = normed.astype(F32)
    arrive(1)
    arms(1, normed)
    total = left_buf[pl.ds(row, 1), :] * right_buf[0:n, :]
    for k in range(1, n):
        total = total + left_buf[pl.ds(k * n + row, 1), :] * right_buf[k * n : (k + 1) * n, :]
    mine = pl.ds(pl.multiple_of(row * n, n), n)
    result = update(1, middle_buf[mine, :], normed_buf[mine, :].astype(BF16), total, same_here)

    picked = lax.broadcasted_iota(jnp.int32, (block, lanes), 1)
    wanted = lax.broadcasted_iota(jnp.int32, (block, lanes), 0) + ch * block
    chosen = jnp.where(picked == wanted, 1.0, 0.0).astype(BF16)
    out_ref[...] = dot_nt(result, chosen).astype(BF16)

    drain(block_buf.at[pl.ds(0, rows * chs - 1)], block_send)
    for t in range(3):
        drain(vector_buf.at[t, pl.ds(0, chs - 1)], vector_send.at[t])
    for u in range(2):
        for t, buf in enumerate((proj_buf, gate_buf, mix_buf)):
            drain(buf.at[u, pl.ds(0, chs - 1)], weight_send.at[u, t])


def window_body(
    rows,
    chs,
    pair_rep,
    residue_mask,
    chain_ids,
    in_gain,
    in_bias,
    w_proj,
    w_gate,
    pair_bias,
    out_gain,
    out_bias,
    w_out,
):
    block, _, n = pair_rep.shape
    lanes = in_gain.shape[1]
    layers, _, parts, _ = w_proj.shape
    vmem = pl.BlockSpec(memory_space=pltpu.VMEM)
    hbm = pl.BlockSpec(memory_space=pl.ANY)
    dma = pltpu.SemaphoreType.DMA
    out = pl.pallas_call(
        functools.partial(window_kernel, rows, chs),
        out_shape=pltpu.VMEM((n, block), BF16),
        in_specs=[hbm] * 11,
        out_specs=vmem,
        scratch_shapes=[
            pltpu.SMEM(residue_mask.shape, jnp.int32),
            pltpu.SMEM(chain_ids.shape, jnp.int32),
            pltpu.VMEM((2, layers, lanes), F32),
            pltpu.VMEM((rows * chs, n, block), BF16),
            pltpu.VMEM((layers, chs, parts * block, lanes), BF16),
            pltpu.VMEM((layers, chs, block, lanes), BF16),
            pltpu.VMEM((layers, chs, block, lanes), BF16),
            pltpu.VMEM((3, chs, layers, block), F32),
            pltpu.VMEM((n * n, lanes), F32),
            pltpu.VMEM((n * n, lanes), F32),
            pltpu.VMEM((n * n, lanes), F32),
            pltpu.VMEM((n * n, lanes), F32),
            pltpu.SemaphoreType.REGULAR((rows,)),
            dma((2,)),
            dma((2,)),
            dma,
            dma,
            dma((3,)),
            dma((3,)),
            dma((layers, 3)),
            dma((layers, 3)),
        ],
        compiler_params=pltpu.CompilerParams(collective_id=0, has_side_effects=True),
    )(
        residue_mask,
        chain_ids,
        jnp.swapaxes(pair_rep[:, 0, :], 0, 1),
        in_gain,
        in_bias,
        jnp.transpose(w_proj, (0, 2, 3, 1)).reshape(layers, parts * block, lanes),
        jnp.swapaxes(w_gate, 1, 2),
        pair_bias,
        out_gain,
        out_bias,
        w_out,
    )
    return jnp.swapaxes(out, 0, 1)[:, None, :]


def channel_norm(values, norm_gain, norm_bias):
    mean_val = jnp.mean(values, axis=0)
    variance = jnp.mean(values * values, axis=0) - mean_val * mean_val
    return (values - mean_val) * lax.rsqrt(variance + epsilon) * norm_gain[
        :, None, None
    ] + norm_bias[:, None, None]


def prepare(
    pair_local, layer, in_gain, in_bias, w_proj, w_gate, pair_bias, mask_rows, mask_cols, same_chain
):
    full_pair = lax.all_gather(pair_local, "ch", axis=0, tiled=True)
    normed = channel_norm(full_pair.astype(jnp.float32), in_gain[layer], in_bias[layer]).astype(
        jnp.bfloat16
    )
    projected = jnp.einsum(
        "cij,cpd->pdij", normed, w_proj[layer], preferred_element_type=jnp.float32
    )
    pair_mask = mask_rows[:, None] * mask_cols[None, :]
    first_arm = (jax.nn.sigmoid(projected[0]) * projected[1] * pair_mask).astype(jnp.bfloat16)
    second_arm = (jax.nn.sigmoid(projected[2]) * projected[3] * pair_mask).astype(jnp.bfloat16)
    logits = jnp.einsum("cij,cd->dij", normed, w_gate[layer], preferred_element_type=jnp.float32)
    logits = logits + pair_bias[layer][:, None, None] * same_chain[None]
    return (first_arm, second_arm, jax.nn.sigmoid(logits))


def finish(product_sum, gating, layer, out_gain, out_bias, w_out):
    totals = lax.psum(
        (jnp.sum(product_sum, axis=0), jnp.sum(product_sum * product_sum, axis=0)), "ch"
    )
    channels = product_sum.shape[0] * lax.axis_size("ch")
    mean_val = totals[0] / channels
    variance = totals[1] / channels - mean_val * mean_val
    scaled = (product_sum - mean_val) * lax.rsqrt(variance + epsilon)
    normed = (scaled * out_gain[layer][:, None, None] + out_bias[layer][:, None, None]).astype(
        jnp.bfloat16
    )
    columns = w_out[layer]
    mixed = lax.psum_scatter(
        jnp.einsum("dij,dc->cij", normed, columns, preferred_element_type=jnp.float32).astype(
            jnp.bfloat16
        ),
        "ch",
        scatter_dimension=0,
        tiled=True,
    ).astype(jnp.float32)
    return gating * mixed


def body(
    pair_rep,
    residue_mask,
    chain_ids,
    in_gain,
    in_bias,
    w_proj,
    w_gate,
    pair_bias,
    out_gain,
    out_bias,
    w_out,
):
    rows_here = pair_rep.shape[1]
    row_start = lax.axis_index("row") * rows_here
    mask_cols = residue_mask.astype(jnp.float32)
    mask_rows = lax.dynamic_slice_in_dim(mask_cols, row_start, rows_here)
    chain_rows = lax.dynamic_slice_in_dim(chain_ids, row_start, rows_here)
    same_chain = (chain_rows[:, None] == chain_ids[None, :]).astype(jnp.float32)
    first_arm, second_arm, gating = prepare(
        pair_rep, 0, in_gain, in_bias, w_proj, w_gate, pair_bias, mask_rows, mask_cols, same_chain
    )
    product_sum = jnp.einsum(
        "cik,cjk->cij",
        first_arm,
        lax.all_gather(second_arm, "row", axis=1, tiled=True),
        preferred_element_type=jnp.float32,
    )
    middle = (
        pair_rep.astype(jnp.float32) + finish(product_sum, gating, 0, out_gain, out_bias, w_out)
    ).astype(jnp.bfloat16)
    in_first, in_second, in_gating = prepare(
        middle, 1, in_gain, in_bias, w_proj, w_gate, pair_bias, mask_rows, mask_cols, same_chain
    )
    exchanged_left = lax.all_to_all(in_first, "row", split_axis=2, concat_axis=1, tiled=True)
    left_rows = jnp.swapaxes(exchanged_left, 1, 2)
    in_product = jnp.einsum(
        "cik,ckj->cij",
        left_rows,
        lax.all_gather(in_second, "row", axis=1, tiled=True),
        preferred_element_type=jnp.float32,
    )
    update = finish(in_product, in_gating, 1, out_gain, out_bias, w_out)
    return (middle.astype(jnp.float32) + update).astype(jnp.bfloat16)


def choose(rows, chs, *args):
    pair_rep, in_gain = args[0], args[3]
    n, lanes = pair_rep.shape[2], in_gain.shape[1]
    one_tile = pair_rep.shape[1] == 1 and n == rows == 8 and lanes == 128
    if one_tile and chs > 1 and args[5].shape[1] == pair_rep.shape[0] * chs:
        return window_body(rows, chs, *args)
    return body(*args)


def solution(mesh):
    return jax.shard_map(
        functools.partial(choose, mesh.shape["row"], mesh.shape["ch"]),
        mesh=mesh,
        in_specs=(
            P("ch", "row", None),
            P(),
            P(),
            P(),
            P(),
            P(None, None, None, "ch"),
            P(None, None, "ch"),
            P(None, "ch"),
            P(None, "ch"),
            P(None, "ch"),
            P(None, "ch", None),
        ),
        out_specs=P("ch", "row", None),
        check_vma=False,
    )
```

```python
import functools
import jax
import jax.numpy as jnp
from jax import lax
from jax.experimental import pallas as pl
from jax.experimental.pallas import tpu as pltpu
from jax.sharding import PartitionSpec as P

epsilon = 1e-05
MESH = pl.DeviceIdType.MESH
F32 = jnp.float32
BF16 = jnp.bfloat16


def lane_norm(values, gain, bias):
    mean_val = jnp.mean(values, axis=-1, keepdims=True)
    variance = jnp.mean(values * values, axis=-1, keepdims=True) - mean_val * mean_val
    return ((values - mean_val) * lax.rsqrt(variance + epsilon) * gain + bias).astype(BF16)


def dot_nt(a, b):
    return lax.dot_general(a, b, (((1,), (1,)), ((), ())), preferred_element_type=F32)


def dot_nn(a, b):
    return lax.dot_general(a, b, (((1,), (0,)), ((), ())), preferred_element_type=F32)


def drain(ref, sem):
    pltpu.make_async_copy(ref, ref, sem).wait()


def window_kernel(
    rows,
    chs,
    mask_hbm,
    chain_hbm,
    pair_hbm,
    in_gain_hbm,
    in_bias_hbm,
    proj_hbm,
    gate_hbm,
    bias_hbm,
    gain_hbm,
    offset_hbm,
    mix_hbm,
    out_ref,
    mask_ref,
    chain_ref,
    norm_buf,
    own_buf,
    block_buf,
    first_buf,
    second_buf,
    last_gate_buf,
    vector_buf,
    left_buf,
    right_buf,
    middle_buf,
    normed_buf,
    near_sem,
    ready_sem,
    scalar_sem,
    norm_sem,
    own_sem,
    block_send,
    block_recv,
    vector_send,
    weight_send,
    parcel_recv,
    far_recv,
    gate_sem,
):
    n = out_ref.shape[0]
    lanes = norm_buf.shape[2]
    block = lanes // chs
    depth = proj_hbm.shape[1]
    row = lax.axis_index("row")
    ch = lax.axis_index("ch")
    here = row * chs + ch

    last = rows - 1
    cores = 2
    partner = ch + 1 - 2 * lax.rem(ch, cores)
    far = [lax.rem(ch + cores * step, chs) for step in range(1, chs // cores)]
    mates = far + [partner]
    is_last = here == rows * chs - 1

    barrier = pltpu.get_barrier_semaphore()

    def greet(r, c):
        pl.semaphore_signal(barrier, inc=1, device_id=(r, c), device_id_type=MESH)

    @pl.when(jnp.logical_not(is_last))
    def _():
        greet(last, chs - 1)

    @pl.when(here < cores)
    def _():
        for m in reversed(range(chs - 1)):
            greet(last, m)

        @pl.loop(1, last)
        def _(back):
            for m in range(chs):
                greet(last - back, m)

        @pl.loop(ch + 1, chs)
        def _(other):
            greet(0, other)

    for mate in mates:

        @pl.when((mate > ch) & (row < last) & (here >= cores))
        def _():
            greet(row, mate)

    lower_mates = lax.rem(ch, cores) + ch // cores
    greeted_above = jnp.minimum(ch, cores) + jnp.where(ch < cores, 0, lower_mates - 1)
    greetings = jnp.where(
        row == 0,
        greeted_above,
        jnp.where(row < last, cores + lower_mates, jnp.where(is_last, rows * chs - 1, cores)),
    )

    pltpu.make_async_copy(pair_hbm, own_buf, own_sem).start()
    pltpu.make_async_copy(pair_hbm, block_buf.at[here], block_recv).start()
    vectors = [
        (ref, vector_buf.at[ch, t], vector_send, 2)
        for t, ref in enumerate((bias_hbm, gain_hbm, offset_hbm))
    ]
    pieces = (
        (0, proj_hbm, first_buf, 0, depth),
        (0, gate_hbm, first_buf, depth, block),
        (0, mix_hbm, first_buf, depth + block, block),
        (1, proj_hbm, second_buf, 0, depth),
        (1, mix_hbm, second_buf, depth, block),
    )
    weights = [
        (ref.at[u], buf.at[ch, pl.ds(at, size)], weight_send.at[u], u)
        for u, ref, buf, at, size in pieces
    ]
    parcels = weights[:3] + vectors + weights[3:]
    for src, dst, _, k in parcels:
        pltpu.make_async_copy(src, dst, parcel_recv.at[k]).start()
    pltpu.make_async_copy(mask_hbm, mask_ref, scalar_sem.at[0]).start()
    pltpu.make_async_copy(chain_hbm, chain_ref, scalar_sem.at[1]).start()
    pltpu.make_async_copy(in_gain_hbm, norm_buf.at[0], norm_sem).start()
    pltpu.make_async_copy(in_bias_hbm, norm_buf.at[1], norm_sem).start()
    pltpu.make_async_copy(gate_hbm.at[1], last_gate_buf, gate_sem).start()

    def send(src, dst, send_sem, recv_sem, r, c):
        pltpu.make_async_remote_copy(
            src_ref=src,
            dst_ref=dst,
            send_sem=send_sem,
            recv_sem=recv_sem,
            device_id=(r, c),
            device_id_type=MESH,
        ).start()

    def send_block(src, r, c):
        send(src, block_buf.at[here], block_send, block_recv, r, c)

    def give(step):
        for src, dst, send_sem, k in parcels:
            recv_sem = far_recv.at[step, k] if step < len(far) else parcel_recv.at[k]
            send(src, dst, send_sem, recv_sem, row, mates[step])

    @pl.when(here > 0)
    def _():
        pl.semaphore_wait(barrier, greetings)

    for m in range(cores):

        @pl.when(here > m)
        def _():
            send_block(pair_hbm, 0, m)

    @pl.when(is_last)
    def _():
        @pl.loop(0, last)
        def _(other):
            for m in range(chs):
                pl.semaphore_signal(ready_sem, inc=1, device_id=(other, m), device_id_type=MESH)

        for m in range(chs - 1):
            pl.semaphore_signal(ready_sem, inc=1, device_id=(last, m), device_id_type=MESH)

    for mate in mates:

        @pl.when((mate < ch) & (row < last))
        def _():
            pl.semaphore_signal(near_sem, inc=1, device_id=(row, mate), device_id_type=MESH)

    for step, mate in enumerate(mates):

        @pl.when((mate < ch) & (row < last))
        def _():
            give(step)

    @pl.when((row < last) & (ch < chs - 1))
    def _():
        pl.semaphore_wait(near_sem, len(mates) - lower_mates)

    @pl.when((row == last) & jnp.logical_not(is_last))
    def _():
        pl.semaphore_wait(ready_sem, 1)

    for step, mate in enumerate(mates):

        @pl.when((mate > ch) | (row == last))
        def _():
            give(step)

    drain(own_buf, own_sem)

    @pl.when(row < last)
    def _():
        pl.semaphore_wait(ready_sem, 1)

    @pl.loop(0, last - row)
    def _(back):
        for m in range(chs):
            send_block(own_buf, last - back, m)

    @pl.loop(1, row)
    def _(other):
        for m in range(chs):
            send_block(own_buf, other, m)

    for m in range(1, chs):

        @pl.when(here < m if m < cores else (here != m))
        def _():
            send_block(own_buf, 0, m)

    @pl.when(row > 0)
    def _():
        for step in range(1, chs):
            send_block(own_buf, row, lax.rem(ch + step, chs))

    parcel_bufs = (first_buf, second_buf, vector_buf)
    parcel_sends = (weight_send.at[0], weight_send.at[1], vector_send)
    for k in (0, 2, 1):
        for step in range(len(far)):
            source = lax.rem(ch + chs - cores * (step + 1), chs)
            piece = parcel_bufs[k].at[source]
            drain(piece, far_recv.at[step, k])
            send(piece, piece, parcel_sends[k], parcel_recv.at[k], row, partner)

    drain(mask_hbm, scalar_sem.at[0])
    drain(chain_hbm, scalar_sem.at[1])
    place = lax.broadcasted_iota(jnp.int32, (n, lanes), 0)
    mask_j = jnp.zeros((n, lanes), jnp.int32)
    chain_j = jnp.zeros((n, lanes), jnp.int32)
    for j in range(n):
        mask_j = jnp.where(place == j, mask_ref[j], mask_j)
        chain_j = jnp.where(place == j, chain_ref[j], chain_j)
    pair_mask = jnp.concatenate([(mask_j * mask_ref[i]).astype(F32) for i in range(n)], axis=0)
    same_chain = jnp.concatenate(
        [jnp.where(chain_j == chain_ref[i], 1.0, 0.0).astype(F32) for i in range(n)], axis=0
    )
    same_here = jnp.where(chain_j == chain_ref[row], 1.0, 0.0).astype(F32)

    def vector(t, u):
        return jnp.concatenate([vector_buf[m, t, u : u + 1, :] for m in range(chs)], axis=1)

    drain(norm_buf, norm_sem)
    drain(vector_buf.at[pl.ds(0, chs - len(far))], parcel_recv.at[2])
    bias = vector(0, 0) * same_chain
    gains = [vector(1, u) for u in range(2)]
    offsets = [vector(2, u) for u in range(2)]
    last_bias = vector_buf[ch, 0, 1:2, :] * same_here[:, 0:block]

    picked = lax.broadcasted_iota(jnp.int32, (block, lanes), 1)
    wanted = lax.broadcasted_iota(jnp.int32, (block, lanes), 0) + ch * block
    chosen = jnp.where(picked == wanted, 1.0, 0.0).astype(BF16)
    drain(last_gate_buf, gate_sem)
    drain(first_buf.at[pl.ds(0, chs - len(far))], parcel_recv.at[0])
    drain(second_buf.at[pl.ds(0, chs - len(far))], parcel_recv.at[1])
    last_mix = dot_nt(second_buf[:, depth:, :].reshape(lanes, lanes), chosen).astype(BF16)

    def arms(buf, normed):
        def value(part):
            part_rows = slice(part * block, (part + 1) * block)
            return dot_nt(normed, buf[:, part_rows, :].reshape(lanes, lanes))

        left = jax.nn.sigmoid(value(0)) * value(1)
        right = jax.nn.sigmoid(value(2)) * value(3)
        left_buf[...] = (left * pair_mask).astype(BF16).astype(F32)
        right_buf[...] = (right * pair_mask).astype(BF16).astype(F32)

    def normalize(u, pair):
        return lane_norm(pair, norm_buf[0, u : u + 1, :], norm_buf[1, u : u + 1, :])

    drain(block_buf, block_recv)
    pair = jnp.concatenate(
        [
            jnp.concatenate([block_buf[i * chs + m].astype(F32) for m in range(chs)], axis=1)
            for i in range(n)
        ],
        axis=0,
    )
    normed = normalize(0, pair)
    logits = dot_nt(normed, first_buf[:, depth : depth + block, :].reshape(lanes, lanes)) + bias
    gating = jax.nn.sigmoid(logits)
    arms(first_buf, normed)
    right_k = [right_buf[pl.ds(k, n, stride=n), :] for k in range(n)]
    product = []
    for i in range(n):
        total = left_buf[i * n : i * n + 1, :] * right_k[0]
        for k in range(1, n):
            total = total + left_buf[i * n + k : i * n + k + 1, :] * right_k[k]
        product.append(total)
    xn = lane_norm(jnp.concatenate(product, axis=0), gains[0], offsets[0])
    mixed = dot_nn(xn, first_buf[:, depth + block :, :].reshape(lanes, lanes))
    middle = (pair + gating * mixed).astype(BF16).astype(F32)
    middle_buf[...] = middle

    normed = normalize(1, middle)
    normed_buf[...] = normed.astype(F32)
    mine = pl.ds(pl.multiple_of(row * n, n), n)
    logits = dot_nt(normed_buf[mine, :].astype(BF16), last_gate_buf[...]) + last_bias
    gating = jax.nn.sigmoid(logits)
    kept = dot_nt(middle_buf[mine, :].astype(BF16), chosen)
    arms(second_buf, normed)
    total = left_buf[pl.ds(row, 1), :] * right_buf[0:n, :]
    for k in range(1, n):
        total = total + left_buf[pl.ds(k * n + row, 1), :] * right_buf[k * n : (k + 1) * n, :]
    xn = lane_norm(total, gains[1], offsets[1])
    out_ref[...] = (kept + gating * dot_nn(xn, last_mix)).astype(BF16)

    drain(block_buf.at[pl.ds(0, rows * chs - 1)], block_send)
    drain(vector_buf.at[pl.ds(0, chs - 1)], vector_send)
    drain(first_buf.at[pl.ds(0, chs - 1)], weight_send.at[0])
    drain(second_buf.at[pl.ds(0, chs - 1)], weight_send.at[1])


def window_body(
    rows,
    chs,
    pair_rep,
    residue_mask,
    chain_ids,
    in_gain,
    in_bias,
    w_proj,
    w_gate,
    pair_bias,
    out_gain,
    out_bias,
    w_out,
):
    block, _, n = pair_rep.shape
    lanes = in_gain.shape[1]
    layers, _, parts, _ = w_proj.shape
    vmem = pl.BlockSpec(memory_space=pltpu.VMEM)
    hbm = pl.BlockSpec(memory_space=pl.ANY)
    dma = pltpu.SemaphoreType.DMA
    out = pl.pallas_call(
        functools.partial(window_kernel, rows, chs),
        out_shape=pltpu.VMEM((n, block), BF16),
        in_specs=[hbm] * 11,
        out_specs=vmem,
        scratch_shapes=[
            pltpu.SMEM(residue_mask.shape, jnp.int32),
            pltpu.SMEM(chain_ids.shape, jnp.int32),
            pltpu.VMEM((2, layers, lanes), F32),
            pltpu.VMEM((n, block), BF16),
            pltpu.VMEM((rows * chs, n, block), BF16),
            pltpu.VMEM((chs, (parts + 2) * block, lanes), BF16),
            pltpu.VMEM((chs, (parts + 1) * block, lanes), BF16),
            pltpu.VMEM((block, lanes), BF16),
            pltpu.VMEM((chs, 3, layers, block), F32),
            pltpu.VMEM((n * n, lanes), F32),
            pltpu.VMEM((n * n, lanes), F32),
            pltpu.VMEM((n * n, lanes), F32),
            pltpu.VMEM((n * n, lanes), F32),
            pltpu.SemaphoreType.REGULAR,
            pltpu.SemaphoreType.REGULAR,
            dma((2,)),
            dma,
            dma,
            dma,
            dma,
            dma,
            dma((2,)),
            dma((3,)),
            dma((chs // 2 - 1, 3)),
            dma,
        ],
        compiler_params=pltpu.CompilerParams(collective_id=0, has_side_effects=True),
    )(
        residue_mask,
        chain_ids,
        jnp.swapaxes(pair_rep[:, 0, :], 0, 1),
        in_gain,
        in_bias,
        jnp.transpose(w_proj, (0, 2, 3, 1)).reshape(layers, parts * block, lanes),
        jnp.swapaxes(w_gate, 1, 2),
        pair_bias,
        out_gain,
        out_bias,
        w_out,
    )
    return jnp.swapaxes(out, 0, 1)[:, None, :]


def channel_norm(values, norm_gain, norm_bias):
    mean_val = jnp.mean(values, axis=0)
    variance = jnp.mean(values * values, axis=0) - mean_val * mean_val
    return (values - mean_val) * lax.rsqrt(variance + epsilon) * norm_gain[
        :, None, None
    ] + norm_bias[:, None, None]


def prepare(
    pair_local, layer, in_gain, in_bias, w_proj, w_gate, pair_bias, mask_rows, mask_cols, same_chain
):
    full_pair = lax.all_gather(pair_local, "ch", axis=0, tiled=True)
    normed = channel_norm(full_pair.astype(jnp.float32), in_gain[layer], in_bias[layer]).astype(
        jnp.bfloat16
    )
    projected = jnp.einsum(
        "cij,cpd->pdij", normed, w_proj[layer], preferred_element_type=jnp.float32
    )
    pair_mask = mask_rows[:, None] * mask_cols[None, :]
    first_arm = (jax.nn.sigmoid(projected[0]) * projected[1] * pair_mask).astype(jnp.bfloat16)
    second_arm = (jax.nn.sigmoid(projected[2]) * projected[3] * pair_mask).astype(jnp.bfloat16)
    logits = jnp.einsum("cij,cd->dij", normed, w_gate[layer], preferred_element_type=jnp.float32)
    logits = logits + pair_bias[layer][:, None, None] * same_chain[None]
    return (first_arm, second_arm, jax.nn.sigmoid(logits))


def finish(product_sum, gating, layer, out_gain, out_bias, w_out):
    totals = lax.psum(
        (jnp.sum(product_sum, axis=0), jnp.sum(product_sum * product_sum, axis=0)), "ch"
    )
    channels = product_sum.shape[0] * lax.axis_size("ch")
    mean_val = totals[0] / channels
    variance = totals[1] / channels - mean_val * mean_val
    scaled = (product_sum - mean_val) * lax.rsqrt(variance + epsilon)
    normed = (scaled * out_gain[layer][:, None, None] + out_bias[layer][:, None, None]).astype(
        jnp.bfloat16
    )
    columns = w_out[layer]
    mixed = lax.psum_scatter(
        jnp.einsum("dij,dc->cij", normed, columns, preferred_element_type=jnp.float32).astype(
            jnp.bfloat16
        ),
        "ch",
        scatter_dimension=0,
        tiled=True,
    ).astype(jnp.float32)
    return gating * mixed


def body(
    pair_rep,
    residue_mask,
    chain_ids,
    in_gain,
    in_bias,
    w_proj,
    w_gate,
    pair_bias,
    out_gain,
    out_bias,
    w_out,
):
    rows_here = pair_rep.shape[1]
    row_start = lax.axis_index("row") * rows_here
    mask_cols = residue_mask.astype(jnp.float32)
    mask_rows = lax.dynamic_slice_in_dim(mask_cols, row_start, rows_here)
    chain_rows = lax.dynamic_slice_in_dim(chain_ids, row_start, rows_here)
    same_chain = (chain_rows[:, None] == chain_ids[None, :]).astype(jnp.float32)
    first_arm, second_arm, gating = prepare(
        pair_rep, 0, in_gain, in_bias, w_proj, w_gate, pair_bias, mask_rows, mask_cols, same_chain
    )
    product_sum = jnp.einsum(
        "cik,cjk->cij",
        first_arm,
        lax.all_gather(second_arm, "row", axis=1, tiled=True),
        preferred_element_type=jnp.float32,
    )
    middle = (
        pair_rep.astype(jnp.float32) + finish(product_sum, gating, 0, out_gain, out_bias, w_out)
    ).astype(jnp.bfloat16)
    in_first, in_second, in_gating = prepare(
        middle, 1, in_gain, in_bias, w_proj, w_gate, pair_bias, mask_rows, mask_cols, same_chain
    )
    exchanged_left = lax.all_to_all(in_first, "row", split_axis=2, concat_axis=1, tiled=True)
    left_rows = jnp.swapaxes(exchanged_left, 1, 2)
    in_product = jnp.einsum(
        "cik,ckj->cij",
        left_rows,
        lax.all_gather(in_second, "row", axis=1, tiled=True),
        preferred_element_type=jnp.float32,
    )
    update = finish(in_product, in_gating, 1, out_gain, out_bias, w_out)
    return (middle.astype(jnp.float32) + update).astype(jnp.bfloat16)


def choose(rows, chs, *args):
    pair_rep, in_gain = args[0], args[3]
    n, lanes = pair_rep.shape[2], in_gain.shape[1]
    one_tile = pair_rep.shape[1] == 1 and n == rows == 8 and lanes == 128
    if one_tile and chs > 2 and chs % 2 == 0 and args[5].shape[1] == pair_rep.shape[0] * chs:
        return window_body(rows, chs, *args)
    return body(*args)


def solution(mesh):
    return jax.shard_map(
        functools.partial(choose, mesh.shape["row"], mesh.shape["ch"]),
        mesh=mesh,
        in_specs=(
            P("ch", "row", None),
            P(),
            P(),
            P(),
            P(),
            P(None, None, None, "ch"),
            P(None, None, "ch"),
            P(None, "ch"),
            P(None, "ch"),
            P(None, "ch"),
            P(None, "ch", None),
        ),
        out_specs=P("ch", "row", None),
        check_vma=False,
    )
```

```python
import functools
import jax
import jax.numpy as jnp
from jax import lax
from jax.experimental import pallas as pl
from jax.experimental.pallas import tpu as pltpu
from jax.sharding import PartitionSpec as P

epsilon = 1e-05
MESH = pl.DeviceIdType.MESH
F32 = jnp.float32
BF16 = jnp.bfloat16


def lane_norm(values, gain, bias):
    mean_val = jnp.mean(values, axis=-1, keepdims=True)
    variance = jnp.mean(values * values, axis=-1, keepdims=True) - mean_val * mean_val
    return ((values - mean_val) * lax.rsqrt(variance + epsilon) * gain + bias).astype(BF16)


def dot_nt(a, b):
    return lax.dot_general(a, b, (((1,), (1,)), ((), ())), preferred_element_type=F32)


def dot_nn(a, b):
    return lax.dot_general(a, b, (((1,), (0,)), ((), ())), preferred_element_type=F32)


def drain(ref, sem):
    pltpu.make_async_copy(ref, ref, sem).wait()


def window_kernel(
    rows,
    chs,
    mask_hbm,
    chain_hbm,
    pair_hbm,
    in_gain_hbm,
    in_bias_hbm,
    proj_hbm,
    gate_hbm,
    bias_hbm,
    gain_hbm,
    offset_hbm,
    mix_hbm,
    out_ref,
    mask_ref,
    chain_ref,
    norm_buf,
    own_buf,
    block_buf,
    first_buf,
    second_buf,
    last_gate_buf,
    vector_buf,
    left_buf,
    right_buf,
    middle_buf,
    near_sem,
    ready_sem,
    scalar_sem,
    norm_sem,
    own_sem,
    block_send,
    block_recv,
    vector_send,
    weight_send,
    parcel_recv,
    far_recv,
    gate_sem,
):
    n = out_ref.shape[0]
    lanes = norm_buf.shape[2]
    block = lanes // chs
    depth = proj_hbm.shape[1]
    row = lax.axis_index("row")
    ch = lax.axis_index("ch")
    here = row * chs + ch

    last = rows - 1
    cores = 2
    partner = ch + 1 - 2 * lax.rem(ch, cores)
    far = [lax.rem(ch + cores * step, chs) for step in range(1, chs // cores)]
    mates = far + [partner]
    is_last = here == rows * chs - 1

    barrier = pltpu.get_barrier_semaphore()

    def greet(r, c):
        pl.semaphore_signal(barrier, inc=1, device_id=(r, c), device_id_type=MESH)

    @pl.when(jnp.logical_not(is_last))
    def _():
        greet(last, chs - 1)

    @pl.when(here < cores)
    def _():
        for m in reversed(range(chs - 1)):
            greet(last, m)

        @pl.loop(1, last)
        def _(back):
            for m in range(chs):
                greet(last - back, m)

        @pl.loop(ch + 1, chs)
        def _(other):
            greet(0, other)

    for mate in mates:

        @pl.when((mate > ch) & (row < last) & (here >= cores))
        def _():
            greet(row, mate)

    lower_mates = lax.rem(ch, cores) + ch // cores
    greeted_above = jnp.minimum(ch, cores) + jnp.where(ch < cores, 0, lower_mates - 1)
    greetings = jnp.where(
        row == 0,
        greeted_above,
        jnp.where(row < last, cores + lower_mates, jnp.where(is_last, rows * chs - 1, cores)),
    )

    pltpu.make_async_copy(pair_hbm, own_buf, own_sem).start()
    pltpu.make_async_copy(pair_hbm, block_buf.at[here], block_recv).start()
    vectors = [
        (ref, vector_buf.at[ch, t], vector_send, 2)
        for t, ref in enumerate((bias_hbm, gain_hbm, offset_hbm))
    ]
    pieces = (
        (0, proj_hbm, first_buf, 0, depth),
        (0, gate_hbm, first_buf, depth, block),
        (0, mix_hbm, first_buf, depth + block, block),
        (1, proj_hbm, second_buf, 0, depth),
        (1, mix_hbm, second_buf, depth, block),
    )
    weights = [
        (ref.at[u], buf.at[ch, pl.ds(at, size)], weight_send.at[u], u)
        for u, ref, buf, at, size in pieces
    ]
    parcels = weights[:3] + vectors + weights[3:]
    for src, dst, _, k in parcels:
        pltpu.make_async_copy(src, dst, parcel_recv.at[k]).start()
    pltpu.make_async_copy(mask_hbm, mask_ref, scalar_sem.at[0]).start()
    pltpu.make_async_copy(chain_hbm, chain_ref, scalar_sem.at[1]).start()
    pltpu.make_async_copy(in_gain_hbm, norm_buf.at[0], norm_sem).start()
    pltpu.make_async_copy(in_bias_hbm, norm_buf.at[1], norm_sem).start()
    pltpu.make_async_copy(gate_hbm.at[1], last_gate_buf, gate_sem).start()

    def send(src, dst, send_sem, recv_sem, r, c):
        pltpu.make_async_remote_copy(
            src_ref=src,
            dst_ref=dst,
            send_sem=send_sem,
            recv_sem=recv_sem,
            device_id=(r, c),
            device_id_type=MESH,
        ).start()

    def send_block(src, r, c):
        send(src, block_buf.at[here], block_send, block_recv, r, c)

    def give(step):
        for src, dst, send_sem, k in parcels:
            recv_sem = far_recv.at[step, k] if step < len(far) else parcel_recv.at[k]
            send(src, dst, send_sem, recv_sem, row, mates[step])

    @pl.when(here > 0)
    def _():
        pl.semaphore_wait(barrier, greetings)

    for m in range(cores):

        @pl.when(here > m)
        def _():
            send_block(pair_hbm, 0, m)

    @pl.when(is_last)
    def _():
        @pl.loop(0, last)
        def _(other):
            for m in range(chs):
                pl.semaphore_signal(ready_sem, inc=1, device_id=(other, m), device_id_type=MESH)

        for m in range(chs - 1):
            pl.semaphore_signal(ready_sem, inc=1, device_id=(last, m), device_id_type=MESH)

    for mate in mates:

        @pl.when((mate < ch) & (row < last))
        def _():
            pl.semaphore_signal(near_sem, inc=1, device_id=(row, mate), device_id_type=MESH)

    for step, mate in enumerate(mates):

        @pl.when((mate < ch) & (row < last))
        def _():
            give(step)

    @pl.when((row < last) & (ch < chs - 1))
    def _():
        pl.semaphore_wait(near_sem, len(mates) - lower_mates)

    @pl.when((row == last) & jnp.logical_not(is_last))
    def _():
        pl.semaphore_wait(ready_sem, 1)

    for step, mate in enumerate(mates):

        @pl.when((mate > ch) | (row == last))
        def _():
            give(step)

    def pass_on():
        for k, buf, send_sem in (
            (0, first_buf, weight_send.at[0]),
            (2, vector_buf, vector_send),
            (1, second_buf, weight_send.at[1]),
        ):
            for step in range(len(far)):
                piece = buf.at[lax.rem(ch + chs - cores * (step + 1), chs)]
                drain(piece, far_recv.at[step, k])
                send(piece, piece, send_sem, parcel_recv.at[k], row, partner)

    drain(own_buf, own_sem)

    @pl.when(here < cores)
    def _():
        pass_on()

    @pl.when(row < last)
    def _():
        pl.semaphore_wait(ready_sem, 1)

    @pl.loop(0, last - row)
    def _(back):
        for m in range(chs):
            send_block(own_buf, last - back, m)

    @pl.loop(1, row)
    def _(other):
        for m in range(chs):
            send_block(own_buf, other, m)

    for m in range(1, chs):

        @pl.when(here < m if m < cores else (here != m))
        def _():
            send_block(own_buf, 0, m)

    @pl.when(row > 0)
    def _():
        for step in range(1, chs):
            send_block(own_buf, row, lax.rem(ch + step, chs))

    @pl.when(here >= cores)
    def _():
        pass_on()

    drain(mask_hbm, scalar_sem.at[0])
    drain(chain_hbm, scalar_sem.at[1])
    place = lax.broadcasted_iota(jnp.int32, (n, lanes), 0)
    mask_j = jnp.zeros((n, lanes), jnp.int32)
    chain_j = jnp.zeros((n, lanes), jnp.int32)
    for j in range(n):
        mask_j = jnp.where(place == j, mask_ref[j], mask_j)
        chain_j = jnp.where(place == j, chain_ref[j], chain_j)
    pair_mask = jnp.concatenate([(mask_j * mask_ref[i]).astype(F32) for i in range(n)], axis=0)
    same_chain = jnp.concatenate(
        [jnp.where(chain_j == chain_ref[i], 1.0, 0.0).astype(F32) for i in range(n)], axis=0
    )
    same_here = jnp.where(chain_j == chain_ref[row], 1.0, 0.0).astype(F32)

    def vector(t, u):
        return jnp.concatenate([vector_buf[m, t, u : u + 1, :] for m in range(chs)], axis=1)

    drain(norm_buf, norm_sem)
    drain(vector_buf.at[pl.ds(0, chs - len(far))], parcel_recv.at[2])
    bias = vector(0, 0) * same_chain
    gains = [vector(1, u) for u in range(2)]
    offsets = [vector(2, u) for u in range(2)]
    last_bias = vector_buf[ch, 0, 1:2, :] * same_here[:, 0:block]

    picked = lax.broadcasted_iota(jnp.int32, (block, lanes), 1)
    wanted = lax.broadcasted_iota(jnp.int32, (block, lanes), 0) + ch * block
    chosen = jnp.where(picked == wanted, 1.0, 0.0).astype(BF16)
    diagonal = lax.broadcasted_iota(jnp.int32, (lanes, lanes), 0) == lax.broadcasted_iota(
        jnp.int32, (lanes, lanes), 1
    )
    def halves(values):
        high = values.astype(BF16)
        return high, (values - high.astype(F32)).astype(BF16)

    def tail_of(*rows_of):
        count = 2 * n
        place_of = lax.broadcasted_iota(jnp.int32, (count, rows_of[0].shape[1]), 0)
        tail = jnp.zeros(place_of.shape, F32)
        for i, values in enumerate(rows_of):
            tail = jnp.where(place_of == i, values.astype(F32), tail)
        return tail.astype(BF16)

    one = jnp.ones((1, lanes), F32)
    in_tails, out_tails = [], []
    for u in range(2):
        ratio = norm_buf[1, u : u + 1, :] / norm_buf[0, u : u + 1, :]
        in_tails.append(tail_of(one, *halves(ratio)))
        ratio = offsets[u] / gains[u]
        out_tails.append(
            tail_of(
                jnp.concatenate([one, 0.0 * one], axis=1), jnp.concatenate(halves(ratio), axis=1)
            )
        )

    def statistics(values):
        mean_val = jnp.mean(values, axis=-1, keepdims=True)
        variance = jnp.mean(values * values, axis=-1, keepdims=True) - mean_val * mean_val
        scale = lax.rsqrt(variance + epsilon)
        return scale, scale * mean_val

    def normed_product(product, stats):
        count = stats[0].shape[0]
        total = product[count : count + 1]
        shift = product[count + 1 : count + 2] + product[count + 2 : count + 3]
        return product[0:count] * stats[0] + (shift - stats[1] * total)

    def fold_in(u, weight):
        return (weight.astype(F32) * norm_buf[0, u : u + 1, :]).astype(BF16)

    def fold_out(u, weight):
        column = jnp.sum(jnp.where(diagonal, gains[u], 0.0), axis=-1, keepdims=True)
        scaled = (weight.astype(F32) * column).astype(BF16)
        return jnp.concatenate([scaled, scaled], axis=0)

    def parts_of(u, buf):
        return [
            fold_in(u, buf[:, part * block : (part + 1) * block, :].reshape(lanes, lanes))
            for part in range(depth // block)
        ]

    def with_tail(values, tail):
        return jnp.concatenate([values, tail], axis=0)

    def arms(lhs, stats, folded):
        value = [normed_product(dot_nt(lhs, part), stats) for part in folded]
        left_buf[...] = (
            (jax.nn.sigmoid(value[0]) * value[1] * pair_mask).astype(BF16).astype(F32)
        )
        right_buf[...] = (
            (jax.nn.sigmoid(value[2]) * value[3] * pair_mask).astype(BF16).astype(F32)
        )

    def mix(u, values, folded):
        both = [half.astype(F32) for half in halves(values)]
        lhs = with_tail(jnp.concatenate(both, axis=1), out_tails[u].astype(F32)).astype(BF16)
        return normed_product(dot_nn(lhs, folded), statistics(values))

    drain(last_gate_buf, gate_sem)
    drain(first_buf.at[pl.ds(0, chs - len(far))], parcel_recv.at[0])
    first_parts = parts_of(0, first_buf)
    first_gate = fold_in(0, first_buf[:, depth : depth + block, :].reshape(lanes, lanes))
    first_mix = fold_out(0, first_buf[:, depth + block :, :].reshape(lanes, lanes))
    drain(second_buf.at[pl.ds(0, chs - len(far))], parcel_recv.at[1])
    second_parts = parts_of(1, second_buf)
    last_gate = fold_in(1, last_gate_buf[...])
    last_mix = fold_out(
        1, dot_nt(second_buf[:, depth:, :].reshape(lanes, lanes), chosen).astype(BF16)
    )

    drain(block_buf, block_recv)
    pair = jnp.concatenate(
        [
            jnp.concatenate([block_buf[i * chs + m].astype(F32) for m in range(chs)], axis=1)
            for i in range(n)
        ],
        axis=0,
    )
    lhs = with_tail(pair.astype(BF16), in_tails[0])
    stats = statistics(pair)
    arms(lhs, stats, first_parts)
    logits = normed_product(dot_nt(lhs, first_gate), stats) + bias
    gating = jax.nn.sigmoid(logits)
    right_k = [right_buf[pl.ds(k, n, stride=n), :] for k in range(n)]
    product = []
    for i in range(n):
        total = left_buf[i * n : i * n + 1, :] * right_k[0]
        for k in range(1, n):
            total = total + left_buf[i * n + k : i * n + k + 1, :] * right_k[k]
        product.append(total)
    mixed = mix(0, jnp.concatenate(product, axis=0), first_mix)
    values = (pair + gating * mixed).astype(BF16)
    middle = values.astype(F32)
    middle_buf[...] = middle

    arms(with_tail(values, in_tails[1]), statistics(middle), second_parts)
    mine = middle_buf[pl.ds(pl.multiple_of(row * n, n), n), :]
    near_lhs = with_tail(mine, in_tails[1].astype(F32)).astype(BF16)
    logits = normed_product(dot_nt(near_lhs, last_gate), statistics(mine))
    gating = jax.nn.sigmoid(logits + last_bias)
    kept = dot_nt(mine.astype(BF16), chosen)
    total = left_buf[pl.ds(row, 1), :] * right_buf[0:n, :]
    for k in range(1, n):
        total = total + left_buf[pl.ds(k * n + row, 1), :] * right_buf[k * n : (k + 1) * n, :]
    out_ref[...] = (kept + gating * mix(1, total, last_mix)).astype(BF16)

    drain(block_buf.at[pl.ds(0, rows * chs - 1)], block_send)
    drain(vector_buf.at[pl.ds(0, chs - 1)], vector_send)
    drain(first_buf.at[pl.ds(0, chs - 1)], weight_send.at[0])
    drain(second_buf.at[pl.ds(0, chs - 1)], weight_send.at[1])


def window_body(
    rows,
    chs,
    pair_rep,
    residue_mask,
    chain_ids,
    in_gain,
    in_bias,
    w_proj,
    w_gate,
    pair_bias,
    out_gain,
    out_bias,
    w_out,
):
    block, _, n = pair_rep.shape
    lanes = in_gain.shape[1]
    layers, _, parts, _ = w_proj.shape
    vmem = pl.BlockSpec(memory_space=pltpu.VMEM)
    hbm = pl.BlockSpec(memory_space=pl.ANY)
    dma = pltpu.SemaphoreType.DMA
    out = pl.pallas_call(
        functools.partial(window_kernel, rows, chs),
        out_shape=pltpu.VMEM((n, block), BF16),
        in_specs=[hbm] * 11,
        out_specs=vmem,
        scratch_shapes=[
            pltpu.SMEM(residue_mask.shape, jnp.int32),
            pltpu.SMEM(chain_ids.shape, jnp.int32),
            pltpu.VMEM((2, layers, lanes), F32),
            pltpu.VMEM((n, block), BF16),
            pltpu.VMEM((rows * chs, n, block), BF16),
            pltpu.VMEM((chs, (parts + 2) * block, lanes), BF16),
            pltpu.VMEM((chs, (parts + 1) * block, lanes), BF16),
            pltpu.VMEM((block, lanes), BF16),
            pltpu.VMEM((chs, 3, layers, block), F32),
            pltpu.VMEM((n * n, lanes), F32),
            pltpu.VMEM((n * n, lanes), F32),
            pltpu.VMEM((n * n, lanes), F32),
            pltpu.SemaphoreType.REGULAR,
            pltpu.SemaphoreType.REGULAR,
            dma((2,)),
            dma,
            dma,
            dma,
            dma,
            dma,
            dma((2,)),
            dma((3,)),
            dma((chs // 2 - 1, 3)),
            dma,
        ],
        compiler_params=pltpu.CompilerParams(collective_id=0, has_side_effects=True),
    )(
        residue_mask,
        chain_ids,
        jnp.swapaxes(pair_rep[:, 0, :], 0, 1),
        in_gain,
        in_bias,
        jnp.transpose(w_proj, (0, 2, 3, 1)).reshape(layers, parts * block, lanes),
        jnp.swapaxes(w_gate, 1, 2),
        pair_bias,
        out_gain,
        out_bias,
        w_out,
    )
    return jnp.swapaxes(out, 0, 1)[:, None, :]


def channel_norm(values, norm_gain, norm_bias):
    mean_val = jnp.mean(values, axis=0)
    variance = jnp.mean(values * values, axis=0) - mean_val * mean_val
    return (values - mean_val) * lax.rsqrt(variance + epsilon) * norm_gain[
        :, None, None
    ] + norm_bias[:, None, None]


def prepare(
    pair_local, layer, in_gain, in_bias, w_proj, w_gate, pair_bias, mask_rows, mask_cols, same_chain
):
    full_pair = lax.all_gather(pair_local, "ch", axis=0, tiled=True)
    normed = channel_norm(full_pair.astype(jnp.float32), in_gain[layer], in_bias[layer]).astype(
        jnp.bfloat16
    )
    projected = jnp.einsum(
        "cij,cpd->pdij", normed, w_proj[layer], preferred_element_type=jnp.float32
    )
    pair_mask = mask_rows[:, None] * mask_cols[None, :]
    first_arm = (jax.nn.sigmoid(projected[0]) * projected[1] * pair_mask).astype(jnp.bfloat16)
    second_arm = (jax.nn.sigmoid(projected[2]) * projected[3] * pair_mask).astype(jnp.bfloat16)
    logits = jnp.einsum("cij,cd->dij", normed, w_gate[layer], preferred_element_type=jnp.float32)
    logits = logits + pair_bias[layer][:, None, None] * same_chain[None]
    return (first_arm, second_arm, jax.nn.sigmoid(logits))


def finish(product_sum, gating, layer, out_gain, out_bias, w_out):
    totals = lax.psum(
        (jnp.sum(product_sum, axis=0), jnp.sum(product_sum * product_sum, axis=0)), "ch"
    )
    channels = product_sum.shape[0] * lax.axis_size("ch")
    mean_val = totals[0] / channels
    variance = totals[1] / channels - mean_val * mean_val
    scaled = (product_sum - mean_val) * lax.rsqrt(variance + epsilon)
    normed = (scaled * out_gain[layer][:, None, None] + out_bias[layer][:, None, None]).astype(
        jnp.bfloat16
    )
    columns = w_out[layer]
    mixed = lax.psum_scatter(
        jnp.einsum("dij,dc->cij", normed, columns, preferred_element_type=jnp.float32).astype(
            jnp.bfloat16
        ),
        "ch",
        scatter_dimension=0,
        tiled=True,
    ).astype(jnp.float32)
    return gating * mixed


def body(
    pair_rep,
    residue_mask,
    chain_ids,
    in_gain,
    in_bias,
    w_proj,
    w_gate,
    pair_bias,
    out_gain,
    out_bias,
    w_out,
):
    rows_here = pair_rep.shape[1]
    row_start = lax.axis_index("row") * rows_here
    mask_cols = residue_mask.astype(jnp.float32)
    mask_rows = lax.dynamic_slice_in_dim(mask_cols, row_start, rows_here)
    chain_rows = lax.dynamic_slice_in_dim(chain_ids, row_start, rows_here)
    same_chain = (chain_rows[:, None] == chain_ids[None, :]).astype(jnp.float32)
    first_arm, second_arm, gating = prepare(
        pair_rep, 0, in_gain, in_bias, w_proj, w_gate, pair_bias, mask_rows, mask_cols, same_chain
    )
    product_sum = jnp.einsum(
        "cik,cjk->cij",
        first_arm,
        lax.all_gather(second_arm, "row", axis=1, tiled=True),
        preferred_element_type=jnp.float32,
    )
    middle = (
        pair_rep.astype(jnp.float32) + finish(product_sum, gating, 0, out_gain, out_bias, w_out)
    ).astype(jnp.bfloat16)
    in_first, in_second, in_gating = prepare(
        middle, 1, in_gain, in_bias, w_proj, w_gate, pair_bias, mask_rows, mask_cols, same_chain
    )
    exchanged_left = lax.all_to_all(in_first, "row", split_axis=2, concat_axis=1, tiled=True)
    left_rows = jnp.swapaxes(exchanged_left, 1, 2)
    in_product = jnp.einsum(
        "cik,ckj->cij",
        left_rows,
        lax.all_gather(in_second, "row", axis=1, tiled=True),
        preferred_element_type=jnp.float32,
    )
    update = finish(in_product, in_gating, 1, out_gain, out_bias, w_out)
    return (middle.astype(jnp.float32) + update).astype(jnp.bfloat16)


def choose(rows, chs, *args):
    pair_rep, in_gain = args[0], args[3]
    n, lanes = pair_rep.shape[2], in_gain.shape[1]
    one_tile = pair_rep.shape[1] == 1 and n == rows == 8 and lanes == 128
    if one_tile and chs > 2 and chs % 2 == 0 and args[5].shape[1] == pair_rep.shape[0] * chs:
        return window_body(rows, chs, *args)
    return body(*args)


def solution(mesh):
    return jax.shard_map(
        functools.partial(choose, mesh.shape["row"], mesh.shape["ch"]),
        mesh=mesh,
        in_specs=(
            P("ch", "row", None),
            P(),
            P(),
            P(),
            P(),
            P(None, None, None, "ch"),
            P(None, None, "ch"),
            P(None, "ch"),
            P(None, "ch"),
            P(None, "ch"),
            P(None, "ch", None),
        ),
        out_specs=P("ch", "row", None),
        check_vma=False,
    )
```

```python
import functools
import jax
import jax.numpy as jnp
from jax import lax
from jax.experimental import pallas as pl
from jax.experimental.pallas import tpu as pltpu
from jax.sharding import PartitionSpec as P

epsilon = 1e-05
MESH = pl.DeviceIdType.MESH
F32 = jnp.float32
BF16 = jnp.bfloat16


def lane_norm(values, gain, bias):
    mean_val = jnp.mean(values, axis=-1, keepdims=True)
    variance = jnp.mean(values * values, axis=-1, keepdims=True) - mean_val * mean_val
    return ((values - mean_val) * lax.rsqrt(variance + epsilon) * gain + bias).astype(BF16)


def dot_nt(a, b):
    return lax.dot_general(a, b, (((1,), (1,)), ((), ())), preferred_element_type=F32)


def dot_nn(a, b):
    return lax.dot_general(a, b, (((1,), (0,)), ((), ())), preferred_element_type=F32)


def drain(ref, sem):
    pltpu.make_async_copy(ref, ref, sem).wait()


def window_kernel(
    rows,
    chs,
    mask_hbm,
    chain_hbm,
    pair_hbm,
    in_gain_hbm,
    in_bias_hbm,
    proj_hbm,
    gate_hbm,
    bias_hbm,
    gain_hbm,
    offset_hbm,
    mix_hbm,
    out_ref,
    mask_ref,
    chain_ref,
    norm_buf,
    own_buf,
    block_buf,
    first_buf,
    second_buf,
    last_gate_buf,
    vector_buf,
    left_buf,
    right_buf,
    middle_buf,
    near_sem,
    ready_sem,
    scalar_sem,
    norm_sem,
    own_sem,
    block_send,
    block_recv,
    vector_send,
    weight_send,
    parcel_recv,
    far_recv,
    gate_sem,
):
    n = out_ref.shape[0]
    lanes = norm_buf.shape[2]
    block = lanes // chs
    depth = proj_hbm.shape[1]
    row = lax.axis_index("row")
    ch = lax.axis_index("ch")
    here = row * chs + ch

    last = rows - 1
    cores = 2
    partner = ch + 1 - 2 * lax.rem(ch, cores)
    far = [lax.rem(ch + cores * step, chs) for step in range(1, chs // cores)]
    mates = far + [partner]
    is_last = here == rows * chs - 1

    barrier = pltpu.get_barrier_semaphore()

    def greet(r, c):
        pl.semaphore_signal(barrier, inc=1, device_id=(r, c), device_id_type=MESH)

    @pl.when(jnp.logical_not(is_last))
    def _():
        greet(last, chs - 1)

    @pl.when(here < cores)
    def _():
        for m in reversed(range(chs - 1)):
            greet(last, m)

        @pl.loop(1, last)
        def _(back):
            for m in range(chs):
                greet(last - back, m)

        @pl.loop(ch + 1, chs)
        def _(other):
            greet(0, other)

    for mate in mates:

        @pl.when((mate > ch) & (row < last) & (here >= cores))
        def _():
            greet(row, mate)

    lower_mates = lax.rem(ch, cores) + ch // cores
    greeted_above = jnp.minimum(ch, cores) + jnp.where(ch < cores, 0, lower_mates - 1)
    greetings = jnp.where(
        row == 0,
        greeted_above,
        jnp.where(row < last, cores + lower_mates, jnp.where(is_last, rows * chs - 1, cores)),
    )

    pltpu.make_async_copy(pair_hbm, own_buf, own_sem).start()
    pltpu.make_async_copy(pair_hbm, block_buf.at[here], block_recv).start()
    vectors = [
        (ref, vector_buf.at[ch, t], vector_send, 2)
        for t, ref in enumerate((bias_hbm, gain_hbm, offset_hbm))
    ]
    pieces = (
        (0, proj_hbm, first_buf, 0, depth),
        (0, gate_hbm, first_buf, depth, block),
        (0, mix_hbm, first_buf, depth + block, block),
        (1, proj_hbm, second_buf, 0, depth),
        (1, mix_hbm, second_buf, depth, block),
    )
    weights = [
        (ref.at[u], buf.at[ch, pl.ds(at, size)], weight_send.at[u], u)
        for u, ref, buf, at, size in pieces
    ]
    parcels = weights[:3] + vectors + weights[3:]
    for src, dst, _, k in parcels:
        pltpu.make_async_copy(src, dst, parcel_recv.at[k]).start()
    pltpu.make_async_copy(mask_hbm, mask_ref, scalar_sem.at[0]).start()
    pltpu.make_async_copy(chain_hbm, chain_ref, scalar_sem.at[1]).start()
    pltpu.make_async_copy(in_gain_hbm, norm_buf.at[0], norm_sem).start()
    pltpu.make_async_copy(in_bias_hbm, norm_buf.at[1], norm_sem).start()
    pltpu.make_async_copy(gate_hbm.at[1], last_gate_buf, gate_sem).start()

    def send(src, dst, send_sem, recv_sem, r, c):
        pltpu.make_async_remote_copy(
            src_ref=src,
            dst_ref=dst,
            send_sem=send_sem,
            recv_sem=recv_sem,
            device_id=(r, c),
            device_id_type=MESH,
        ).start()

    def send_block(src, r, c):
        send(src, block_buf.at[here], block_send, block_recv, r, c)

    def give(step):
        for src, dst, send_sem, k in parcels:
            recv_sem = far_recv.at[step, k] if step < len(far) else parcel_recv.at[k]
            send(src, dst, send_sem, recv_sem, row, mates[step])

    @pl.when(here > 0)
    def _():
        pl.semaphore_wait(barrier, greetings)

    for m in range(cores):

        @pl.when(here > m)
        def _():
            send_block(pair_hbm, 0, m)

    @pl.when(is_last)
    def _():
        @pl.loop(0, last)
        def _(other):
            for m in range(chs):
                pl.semaphore_signal(ready_sem, inc=1, device_id=(other, m), device_id_type=MESH)

        for m in range(chs - 1):
            pl.semaphore_signal(ready_sem, inc=1, device_id=(last, m), device_id_type=MESH)

    for mate in mates:

        @pl.when((mate < ch) & (row < last))
        def _():
            pl.semaphore_signal(near_sem, inc=1, device_id=(row, mate), device_id_type=MESH)

    for step, mate in enumerate(mates):

        @pl.when((mate < ch) & (row < last))
        def _():
            give(step)

    @pl.when((row < last) & (ch < chs - 1))
    def _():
        pl.semaphore_wait(near_sem, len(mates) - lower_mates)

    @pl.when((row == last) & jnp.logical_not(is_last))
    def _():
        pl.semaphore_wait(ready_sem, 1)

    for step, mate in enumerate(mates):

        @pl.when((mate > ch) | (row == last))
        def _():
            give(step)

    def pass_on():
        for k, buf, send_sem in (
            (0, first_buf, weight_send.at[0]),
            (2, vector_buf, vector_send),
            (1, second_buf, weight_send.at[1]),
        ):
            for step in range(len(far)):
                piece = buf.at[lax.rem(ch + chs - cores * (step + 1), chs)]
                drain(piece, far_recv.at[step, k])
                send(piece, piece, send_sem, parcel_recv.at[k], row, partner)

    drain(own_buf, own_sem)

    @pl.when(here < cores)
    def _():
        pass_on()

    @pl.when(row < last)
    def _():
        pl.semaphore_wait(ready_sem, 1)

    @pl.loop(0, last - row)
    def _(back):
        for m in range(chs):
            send_block(own_buf, last - back, m)

    @pl.loop(1, row)
    def _(other):
        for m in range(chs):
            send_block(own_buf, other, m)

    for m in range(1, chs):

        @pl.when(here < m if m < cores else (here != m))
        def _():
            send_block(own_buf, 0, m)

    @pl.when(row > 0)
    def _():
        for step in range(1, chs):
            send_block(own_buf, row, lax.rem(ch + step, chs))

    @pl.when(here >= cores)
    def _():
        pass_on()

    drain(mask_hbm, scalar_sem.at[0])
    drain(chain_hbm, scalar_sem.at[1])
    place = lax.broadcasted_iota(jnp.int32, (n, lanes), 0)
    mask_j = jnp.zeros((n, lanes), jnp.int32)
    chain_j = jnp.zeros((n, lanes), jnp.int32)
    for j in range(n):
        mask_j = jnp.where(place == j, mask_ref[j], mask_j)
        chain_j = jnp.where(place == j, chain_ref[j], chain_j)
    pair_mask = jnp.concatenate([(mask_j * mask_ref[i]).astype(F32) for i in range(n)], axis=0)
    same_chain = jnp.concatenate(
        [jnp.where(chain_j == chain_ref[i], 1.0, 0.0).astype(F32) for i in range(n)], axis=0
    )
    same_here = jnp.where(chain_j == chain_ref[row], 1.0, 0.0).astype(F32)

    def vector(t, u):
        return jnp.concatenate([vector_buf[m, t, u : u + 1, :] for m in range(chs)], axis=1)

    drain(norm_buf, norm_sem)
    drain(vector_buf.at[pl.ds(0, chs - len(far))], parcel_recv.at[2])
    bias = vector(0, 0) * same_chain
    gains = [vector(1, u) for u in range(2)]
    offsets = [vector(2, u) for u in range(2)]
    last_bias = vector_buf[ch, 0, 1:2, :] * same_here[:, 0:block]

    picked = lax.broadcasted_iota(jnp.int32, (block, lanes), 1)
    wanted = lax.broadcasted_iota(jnp.int32, (block, lanes), 0) + ch * block
    chosen = jnp.where(picked == wanted, 1.0, 0.0).astype(BF16)
    diagonal = lax.broadcasted_iota(jnp.int32, (lanes, lanes), 0) == lax.broadcasted_iota(
        jnp.int32, (lanes, lanes), 1
    )
    def halves(values):
        high = values.astype(BF16)
        return high, (values - high.astype(F32)).astype(BF16)

    def tail_of(*rows_of):
        count = 2 * n
        place_of = lax.broadcasted_iota(jnp.int32, (count, rows_of[0].shape[1]), 0)
        tail = jnp.zeros(place_of.shape, F32)
        for i, values in enumerate(rows_of):
            tail = jnp.where(place_of == i, values.astype(F32), tail)
        return tail.astype(BF16)

    one = jnp.ones((1, lanes), F32)
    in_tails, out_tails = [], []
    for u in range(2):
        ratio = norm_buf[1, u : u + 1, :] / norm_buf[0, u : u + 1, :]
        in_tails.append(tail_of(one, *halves(ratio)))
        out_tails.append(tail_of(one, *halves(offsets[u] / gains[u])))

    def statistics(values):
        mean_val = jnp.mean(values, axis=-1, keepdims=True)
        variance = jnp.mean(values * values, axis=-1, keepdims=True) - mean_val * mean_val
        scale = lax.rsqrt(variance + epsilon)
        return scale, scale * mean_val

    def sigmoid(values):
        return 0.5 * jnp.tanh(0.5 * values) + 0.5

    def fold(dot, scaled, tail):
        product = dot(tail, scaled)
        return scaled, product[0:1], product[1:2] + product[2:3]

    def normed_product(product, stats, folded):
        return product * stats[0] + (folded[2] - stats[1] * folded[1])

    def fold_in(u, weight):
        scaled = (weight.astype(F32) * norm_buf[0, u : u + 1, :]).astype(BF16)
        return fold(dot_nt, scaled, in_tails[u])

    def fold_out(u, weight):
        column = jnp.sum(jnp.where(diagonal, gains[u], 0.0), axis=-1, keepdims=True)
        scaled = (weight.astype(F32) * column).astype(BF16)
        return fold(dot_nn, scaled, out_tails[u])

    def parts_of(u, buf):
        return [
            fold_in(u, buf[:, part * block : (part + 1) * block, :].reshape(lanes, lanes))
            for part in range(depth // block)
        ]

    def arms(values, stats, folded):
        value = [normed_product(dot_nt(values, part[0]), stats, part) for part in folded]
        left_buf[...] = sigmoid(value[0]) * (value[1] * pair_mask)
        right_buf[...] = sigmoid(value[2]) * (value[3] * pair_mask)

    def mix(values, folded):
        both = jnp.concatenate(halves(values), axis=1)
        product = dot_nn(both, jnp.concatenate([folded[0], folded[0]], axis=0))
        return normed_product(product, statistics(values), folded)

    drain(last_gate_buf, gate_sem)
    drain(first_buf.at[pl.ds(0, chs - len(far))], parcel_recv.at[0])
    first_parts = parts_of(0, first_buf)
    first_gate = fold_in(0, first_buf[:, depth : depth + block, :].reshape(lanes, lanes))
    first_mix = fold_out(0, first_buf[:, depth + block :, :].reshape(lanes, lanes))
    drain(second_buf.at[pl.ds(0, chs - len(far))], parcel_recv.at[1])
    second_parts = parts_of(1, second_buf)
    last_gate = fold_in(1, last_gate_buf[...])
    last_mix = fold_out(
        1, dot_nt(second_buf[:, depth:, :].reshape(lanes, lanes), chosen).astype(BF16)
    )

    drain(block_buf, block_recv)
    pair = jnp.concatenate(
        [
            jnp.concatenate([block_buf[i * chs + m].astype(F32) for m in range(chs)], axis=1)
            for i in range(n)
        ],
        axis=0,
    )
    values = pair.astype(BF16)
    stats = statistics(pair)
    arms(values, stats, first_parts)
    gating = sigmoid(normed_product(dot_nt(values, first_gate[0]), stats, first_gate) + bias)
    right_k = [right_buf[pl.ds(k, n, stride=n), :] for k in range(n)]
    product = []
    for i in range(n):
        total = left_buf[i * n : i * n + 1, :] * right_k[0]
        for k in range(1, n):
            total = total + left_buf[i * n + k : i * n + k + 1, :] * right_k[k]
        product.append(total)
    mixed = mix(jnp.concatenate(product, axis=0), first_mix)
    values = (pair + gating * mixed).astype(BF16)
    middle = values.astype(F32)
    middle_buf[...] = middle

    arms(values, statistics(middle), second_parts)
    mine = middle_buf[pl.ds(pl.multiple_of(row * n, n), n), :]
    logits = normed_product(dot_nt(mine.astype(BF16), last_gate[0]), statistics(mine), last_gate)
    gating = sigmoid(logits + last_bias)
    kept = dot_nt(mine.astype(BF16), chosen)
    total = left_buf[pl.ds(row, 1), :] * right_buf[0:n, :]
    for k in range(1, n):
        total = total + left_buf[pl.ds(k * n + row, 1), :] * right_buf[k * n : (k + 1) * n, :]
    out_ref[...] = (kept + gating * mix(total, last_mix)).astype(BF16)

    drain(block_buf.at[pl.ds(0, rows * chs - 1)], block_send)
    drain(vector_buf.at[pl.ds(0, chs - 1)], vector_send)
    drain(first_buf.at[pl.ds(0, chs - 1)], weight_send.at[0])
    drain(second_buf.at[pl.ds(0, chs - 1)], weight_send.at[1])


def window_body(
    rows,
    chs,
    pair_rep,
    residue_mask,
    chain_ids,
    in_gain,
    in_bias,
    w_proj,
    w_gate,
    pair_bias,
    out_gain,
    out_bias,
    w_out,
):
    block, _, n = pair_rep.shape
    lanes = in_gain.shape[1]
    layers, _, parts, _ = w_proj.shape
    vmem = pl.BlockSpec(memory_space=pltpu.VMEM)
    hbm = pl.BlockSpec(memory_space=pl.ANY)
    dma = pltpu.SemaphoreType.DMA
    out = pl.pallas_call(
        functools.partial(window_kernel, rows, chs),
        out_shape=pltpu.VMEM((n, block), BF16),
        in_specs=[hbm] * 11,
        out_specs=vmem,
        scratch_shapes=[
            pltpu.SMEM(residue_mask.shape, jnp.int32),
            pltpu.SMEM(chain_ids.shape, jnp.int32),
            pltpu.VMEM((2, layers, lanes), F32),
            pltpu.VMEM((n, block), BF16),
            pltpu.VMEM((rows * chs, n, block), BF16),
            pltpu.VMEM((chs, (parts + 2) * block, lanes), BF16),
            pltpu.VMEM((chs, (parts + 1) * block, lanes), BF16),
            pltpu.VMEM((block, lanes), BF16),
            pltpu.VMEM((chs, 3, layers, block), F32),
            pltpu.VMEM((n * n, lanes), F32),
            pltpu.VMEM((n * n, lanes), F32),
            pltpu.VMEM((n * n, lanes), F32),
            pltpu.SemaphoreType.REGULAR,
            pltpu.SemaphoreType.REGULAR,
            dma((2,)),
            dma,
            dma,
            dma,
            dma,
            dma,
            dma((2,)),
            dma((3,)),
            dma((chs // 2 - 1, 3)),
            dma,
        ],
        compiler_params=pltpu.CompilerParams(collective_id=0, has_side_effects=True),
    )(
        residue_mask,
        chain_ids,
        jnp.swapaxes(pair_rep[:, 0, :], 0, 1),
        in_gain,
        in_bias,
        jnp.transpose(w_proj, (0, 2, 3, 1)).reshape(layers, parts * block, lanes),
        jnp.swapaxes(w_gate, 1, 2),
        pair_bias,
        out_gain,
        out_bias,
        w_out,
    )
    return jnp.swapaxes(out, 0, 1)[:, None, :]


def channel_norm(values, norm_gain, norm_bias):
    mean_val = jnp.mean(values, axis=0)
    variance = jnp.mean(values * values, axis=0) - mean_val * mean_val
    return (values - mean_val) * lax.rsqrt(variance + epsilon) * norm_gain[
        :, None, None
    ] + norm_bias[:, None, None]


def prepare(
    pair_local, layer, in_gain, in_bias, w_proj, w_gate, pair_bias, mask_rows, mask_cols, same_chain
):
    full_pair = lax.all_gather(pair_local, "ch", axis=0, tiled=True)
    normed = channel_norm(full_pair.astype(jnp.float32), in_gain[layer], in_bias[layer]).astype(
        jnp.bfloat16
    )
    projected = jnp.einsum(
        "cij,cpd->pdij", normed, w_proj[layer], preferred_element_type=jnp.float32
    )
    pair_mask = mask_rows[:, None] * mask_cols[None, :]
    first_arm = (jax.nn.sigmoid(projected[0]) * projected[1] * pair_mask).astype(jnp.bfloat16)
    second_arm = (jax.nn.sigmoid(projected[2]) * projected[3] * pair_mask).astype(jnp.bfloat16)
    logits = jnp.einsum("cij,cd->dij", normed, w_gate[layer], preferred_element_type=jnp.float32)
    logits = logits + pair_bias[layer][:, None, None] * same_chain[None]
    return (first_arm, second_arm, jax.nn.sigmoid(logits))


def finish(product_sum, gating, layer, out_gain, out_bias, w_out):
    totals = lax.psum(
        (jnp.sum(product_sum, axis=0), jnp.sum(product_sum * product_sum, axis=0)), "ch"
    )
    channels = product_sum.shape[0] * lax.axis_size("ch")
    mean_val = totals[0] / channels
    variance = totals[1] / channels - mean_val * mean_val
    scaled = (product_sum - mean_val) * lax.rsqrt(variance + epsilon)
    normed = (scaled * out_gain[layer][:, None, None] + out_bias[layer][:, None, None]).astype(
        jnp.bfloat16
    )
    columns = w_out[layer]
    mixed = lax.psum_scatter(
        jnp.einsum("dij,dc->cij", normed, columns, preferred_element_type=jnp.float32).astype(
            jnp.bfloat16
        ),
        "ch",
        scatter_dimension=0,
        tiled=True,
    ).astype(jnp.float32)
    return gating * mixed


def body(
    pair_rep,
    residue_mask,
    chain_ids,
    in_gain,
    in_bias,
    w_proj,
    w_gate,
    pair_bias,
    out_gain,
    out_bias,
    w_out,
):
    rows_here = pair_rep.shape[1]
    row_start = lax.axis_index("row") * rows_here
    mask_cols = residue_mask.astype(jnp.float32)
    mask_rows = lax.dynamic_slice_in_dim(mask_cols, row_start, rows_here)
    chain_rows = lax.dynamic_slice_in_dim(chain_ids, row_start, rows_here)
    same_chain = (chain_rows[:, None] == chain_ids[None, :]).astype(jnp.float32)
    first_arm, second_arm, gating = prepare(
        pair_rep, 0, in_gain, in_bias, w_proj, w_gate, pair_bias, mask_rows, mask_cols, same_chain
    )
    product_sum = jnp.einsum(
        "cik,cjk->cij",
        first_arm,
        lax.all_gather(second_arm, "row", axis=1, tiled=True),
        preferred_element_type=jnp.float32,
    )
    middle = (
        pair_rep.astype(jnp.float32) + finish(product_sum, gating, 0, out_gain, out_bias, w_out)
    ).astype(jnp.bfloat16)
    in_first, in_second, in_gating = prepare(
        middle, 1, in_gain, in_bias, w_proj, w_gate, pair_bias, mask_rows, mask_cols, same_chain
    )
    exchanged_left = lax.all_to_all(in_first, "row", split_axis=2, concat_axis=1, tiled=True)
    left_rows = jnp.swapaxes(exchanged_left, 1, 2)
    in_product = jnp.einsum(
        "cik,ckj->cij",
        left_rows,
        lax.all_gather(in_second, "row", axis=1, tiled=True),
        preferred_element_type=jnp.float32,
    )
    update = finish(in_product, in_gating, 1, out_gain, out_bias, w_out)
    return (middle.astype(jnp.float32) + update).astype(jnp.bfloat16)


def choose(rows, chs, *args):
    pair_rep, in_gain = args[0], args[3]
    n, lanes = pair_rep.shape[2], in_gain.shape[1]
    one_tile = pair_rep.shape[1] == 1 and n == rows == 8 and lanes == 128
    if one_tile and chs > 2 and chs % 2 == 0 and args[5].shape[1] == pair_rep.shape[0] * chs:
        return window_body(rows, chs, *args)
    return body(*args)


def solution(mesh):
    return jax.shard_map(
        functools.partial(choose, mesh.shape["row"], mesh.shape["ch"]),
        mesh=mesh,
        in_specs=(
            P("ch", "row", None),
            P(),
            P(),
            P(),
            P(),
            P(None, None, None, "ch"),
            P(None, None, "ch"),
            P(None, "ch"),
            P(None, "ch"),
            P(None, "ch"),
            P(None, "ch", None),
        ),
        out_specs=P("ch", "row", None),
        check_vma=False,
    )
```

```python
import functools
import jax
import jax.numpy as jnp
from jax import lax
from jax.experimental import pallas as pl
from jax.experimental.pallas import tpu as pltpu
from jax.sharding import PartitionSpec as P

epsilon = 1e-05
MESH = pl.DeviceIdType.MESH
F32 = jnp.float32
BF16 = jnp.bfloat16


def lane_norm(values, gain, bias):
    mean_val = jnp.mean(values, axis=-1, keepdims=True)
    variance = jnp.mean(values * values, axis=-1, keepdims=True) - mean_val * mean_val
    return ((values - mean_val) * lax.rsqrt(variance + epsilon) * gain + bias).astype(BF16)


def dot_nt(a, b):
    return lax.dot_general(a, b, (((1,), (1,)), ((), ())), preferred_element_type=F32)


def dot_nn(a, b):
    return lax.dot_general(a, b, (((1,), (0,)), ((), ())), preferred_element_type=F32)


def drain(ref, sem):
    pltpu.make_async_copy(ref, ref, sem).wait()


def window_kernel(
    rows,
    chs,
    mask_hbm,
    chain_hbm,
    pair_hbm,
    in_gain_hbm,
    in_bias_hbm,
    proj_hbm,
    gate_hbm,
    bias_hbm,
    gain_hbm,
    offset_hbm,
    mix_hbm,
    out_ref,
    mask_ref,
    chain_ref,
    norm_buf,
    own_buf,
    block_buf,
    first_buf,
    second_buf,
    last_gate_buf,
    vector_buf,
    left_buf,
    right_buf,
    middle_buf,
    near_sem,
    ready_sem,
    scalar_sem,
    norm_sem,
    own_sem,
    block_send,
    block_recv,
    vector_send,
    weight_send,
    parcel_recv,
    far_recv,
    gate_sem,
):
    n = out_ref.shape[0]
    lanes = norm_buf.shape[2]
    block = lanes // chs
    depth = proj_hbm.shape[1]
    row = lax.axis_index("row")
    ch = lax.axis_index("ch")
    here = row * chs + ch

    last = rows - 1
    cores = 2
    partner = ch + 1 - 2 * lax.rem(ch, cores)
    far = [lax.rem(ch + cores * step, chs) for step in range(1, chs // cores)]
    mates = far + [partner]
    is_last = here == rows * chs - 1

    barrier = pltpu.get_barrier_semaphore()

    def greet(r, c):
        pl.semaphore_signal(barrier, inc=1, device_id=(r, c), device_id_type=MESH)

    @pl.when(jnp.logical_not(is_last))
    def _():
        greet(last, chs - 1)

    @pl.when(here < cores)
    def _():
        for m in reversed(range(chs - 1)):
            greet(last, m)

        @pl.loop(1, last)
        def _(back):
            for m in range(chs):
                greet(last - back, m)

        @pl.loop(ch + 1, chs)
        def _(other):
            greet(0, other)

    for mate in mates:

        @pl.when((mate > ch) & (row < last) & (here >= cores))
        def _():
            greet(row, mate)

    lower_mates = lax.rem(ch, cores) + ch // cores
    greeted_above = jnp.minimum(ch, cores) + jnp.where(ch < cores, 0, lower_mates - 1)
    greetings = jnp.where(
        row == 0,
        greeted_above,
        jnp.where(row < last, cores + lower_mates, jnp.where(is_last, rows * chs - 1, cores)),
    )

    def send(src, dst, send_sem, recv_sem, r, c):
        pltpu.make_async_remote_copy(
            src_ref=src,
            dst_ref=dst,
            send_sem=send_sem,
            recv_sem=recv_sem,
            device_id=(r, c),
            device_id_type=MESH,
        ).start()

    def send_block(src, r, c):
        send(src, block_buf.at[ch * rows + row], block_send, block_recv, r, c)

    @pl.when(here > 0)
    def _():
        pl.semaphore_wait(barrier, greetings)

    for m in range(cores):

        @pl.when(here > m)
        def _():
            send_block(pair_hbm, 0, m)

    @pl.when(is_last)
    def _():
        @pl.loop(0, last)
        def _(other):
            for m in range(chs):
                pl.semaphore_signal(ready_sem, inc=1, device_id=(other, m), device_id_type=MESH)

        for m in range(chs - 1):
            pl.semaphore_signal(ready_sem, inc=1, device_id=(last, m), device_id_type=MESH)

    for mate in mates:

        @pl.when((mate < ch) & (row < last))
        def _():
            pl.semaphore_signal(near_sem, inc=1, device_id=(row, mate), device_id_type=MESH)

    pltpu.make_async_copy(pair_hbm, own_buf, own_sem).start()
    pltpu.make_async_copy(pair_hbm, block_buf.at[ch * rows + row], block_recv).start()
    vectors = [
        (ref, vector_buf.at[ch, t], vector_send, 2)
        for t, ref in enumerate((bias_hbm, gain_hbm, offset_hbm))
    ]
    pieces = (
        (0, proj_hbm, first_buf, 0, depth),
        (0, gate_hbm, first_buf, depth, block),
        (0, mix_hbm, first_buf, depth + block, block),
        (1, proj_hbm, second_buf, 0, depth),
        (1, mix_hbm, second_buf, depth, block),
    )
    weights = [
        (ref.at[u], buf.at[ch, pl.ds(at, size)], weight_send.at[u], u)
        for u, ref, buf, at, size in pieces
    ]
    parcels = weights[:3] + vectors + weights[3:]
    for src, dst, _, k in parcels:
        pltpu.make_async_copy(src, dst, parcel_recv.at[k]).start()
    pltpu.make_async_copy(mask_hbm, mask_ref, scalar_sem.at[0]).start()
    pltpu.make_async_copy(chain_hbm, chain_ref, scalar_sem.at[1]).start()
    pltpu.make_async_copy(in_gain_hbm, norm_buf.at[0], norm_sem).start()
    pltpu.make_async_copy(in_bias_hbm, norm_buf.at[1], norm_sem).start()
    pltpu.make_async_copy(gate_hbm.at[1], last_gate_buf, gate_sem).start()

    def give(step):
        for src, dst, send_sem, k in parcels:
            recv_sem = far_recv.at[step, k] if step < len(far) else parcel_recv.at[k]
            send(src, dst, send_sem, recv_sem, row, mates[step])

    for step, mate in enumerate(mates):

        @pl.when((mate < ch) & (row < last))
        def _():
            give(step)

    @pl.when((row < last) & (ch < chs - 1))
    def _():
        pl.semaphore_wait(near_sem, len(mates) - lower_mates)

    @pl.when((row == last) & jnp.logical_not(is_last))
    def _():
        pl.semaphore_wait(ready_sem, 1)

    for step, mate in enumerate(mates):

        @pl.when((mate > ch) | (row == last))
        def _():
            give(step)

    def pass_on():
        for k, buf, send_sem in (
            (0, first_buf, weight_send.at[0]),
            (2, vector_buf, vector_send),
            (1, second_buf, weight_send.at[1]),
        ):
            for step in range(len(far)):
                piece = buf.at[lax.rem(ch + chs - cores * (step + 1), chs)]
                drain(piece, far_recv.at[step, k])
                send(piece, piece, send_sem, parcel_recv.at[k], row, partner)

    drain(own_buf, own_sem)

    @pl.when(here < cores)
    def _():
        pass_on()

    @pl.when(row < last)
    def _():
        pl.semaphore_wait(ready_sem, 1)

    for m in reversed(range(1, chs)):

        @pl.when(here < m if m < cores else (here != m))
        def _():
            send_block(own_buf, 0, m)

    @pl.when(row > 0)
    def _():
        for step in range(1, chs):
            send_block(own_buf, row, lax.rem(ch + step, chs))

    @pl.loop(1, row)
    def _(other):
        for m in reversed(range(chs)):
            send_block(own_buf, other, m)

    @pl.loop(row + 1, rows)
    def _(other):
        for m in reversed(range(chs)):
            send_block(own_buf, other, m)

    @pl.when(here >= cores)
    def _():
        pass_on()

    drain(mask_hbm, scalar_sem.at[0])
    drain(chain_hbm, scalar_sem.at[1])
    place = lax.broadcasted_iota(jnp.int32, (n, lanes), 0)
    mask_j = jnp.zeros((n, lanes), jnp.int32)
    chain_j = jnp.zeros((n, lanes), jnp.int32)
    for j in range(n):
        mask_j = jnp.where(place == j, mask_ref[j], mask_j)
        chain_j = jnp.where(place == j, chain_ref[j], chain_j)
    pair_mask = jnp.concatenate([(mask_j * mask_ref[i]).astype(F32) for i in range(n)], axis=0)
    same_chain = jnp.concatenate(
        [jnp.where(chain_j == chain_ref[i], 1.0, 0.0).astype(F32) for i in range(n)], axis=0
    )
    same_here = jnp.where(chain_j == chain_ref[row], 1.0, 0.0).astype(F32)

    def vector(t, u):
        return jnp.concatenate([vector_buf[m, t, u : u + 1, :] for m in range(chs)], axis=1)

    drain(norm_buf, norm_sem)
    drain(vector_buf.at[pl.ds(0, chs - len(far))], parcel_recv.at[2])
    bias = vector(0, 0) * same_chain
    gains = [vector(1, u) for u in range(2)]
    offsets = [vector(2, u) for u in range(2)]
    last_bias = vector_buf[ch, 0, 1:2, :] * same_here[:, 0:block]

    picked = lax.broadcasted_iota(jnp.int32, (block, lanes), 1)
    wanted = lax.broadcasted_iota(jnp.int32, (block, lanes), 0) + ch * block
    chosen = jnp.where(picked == wanted, 1.0, 0.0).astype(BF16)
    diagonal = lax.broadcasted_iota(jnp.int32, (lanes, lanes), 0) == lax.broadcasted_iota(
        jnp.int32, (lanes, lanes), 1
    )
    def halves(values):
        high = values.astype(BF16)
        return high, (values - high.astype(F32)).astype(BF16)

    def tail_of(*rows_of):
        count = 2 * n
        place_of = lax.broadcasted_iota(jnp.int32, (count, rows_of[0].shape[1]), 0)
        tail = jnp.zeros(place_of.shape, F32)
        for i, values in enumerate(rows_of):
            tail = jnp.where(place_of == i, values.astype(F32), tail)
        return tail.astype(BF16)

    one = jnp.ones((1, lanes), F32)
    in_tails, out_tails = [], []
    for u in range(2):
        ratio = norm_buf[1, u : u + 1, :] / norm_buf[0, u : u + 1, :]
        in_tails.append(tail_of(one, *halves(ratio)))
        out_tails.append(tail_of(one, *halves(offsets[u] / gains[u])))

    def statistics(values):
        mean_val = jnp.mean(values, axis=-1, keepdims=True)
        variance = jnp.mean(values * values, axis=-1, keepdims=True) - mean_val * mean_val
        scale = lax.rsqrt(variance + epsilon)
        return scale, scale * mean_val

    def sigmoid(values):
        return 0.5 * jnp.tanh(0.5 * values) + 0.5

    def fold(dot, scaled, tail):
        product = dot(tail, scaled)
        return scaled, product[0:1], product[1:2] + product[2:3]

    def normed_product(product, stats, folded):
        return product * stats[0] + (folded[2] - stats[1] * folded[1])

    def fold_in(u, weight):
        scaled = (weight.astype(F32) * norm_buf[0, u : u + 1, :]).astype(BF16)
        return fold(dot_nt, scaled, in_tails[u])

    def fold_out(u, weight):
        column = jnp.sum(jnp.where(diagonal, gains[u], 0.0), axis=-1, keepdims=True)
        scaled = (weight.astype(F32) * column).astype(BF16)
        return fold(dot_nn, scaled, out_tails[u])

    def parts_of(u, buf):
        weights = [
            buf[:, part * block : (part + 1) * block, :].reshape(lanes, lanes)
            for part in range(depth // block)
        ]
        return [
            fold_in(u, jnp.concatenate(weights[first : first + 4], axis=0))
            for first in range(0, len(weights), 4)
        ]

    def arms(values, stats, folded):
        value = [normed_product(dot_nt(values, part[0]), stats, part) for part in folded]
        value = [
            wide[:, first : first + lanes]
            for wide in value
            for first in range(0, wide.shape[1], lanes)
        ]
        left_buf[...] = sigmoid(value[0]) * (value[1] * pair_mask)
        right_buf[...] = sigmoid(value[2]) * (value[3] * pair_mask)

    def mix(values, folded):
        both = jnp.concatenate(halves(values), axis=1)
        product = dot_nn(both, jnp.concatenate([folded[0], folded[0]], axis=0))
        return normed_product(product, statistics(values), folded)

    drain(last_gate_buf, gate_sem)
    drain(first_buf.at[pl.ds(0, chs - len(far))], parcel_recv.at[0])
    first_parts = parts_of(0, first_buf)
    first_gate = fold_in(0, first_buf[:, depth : depth + block, :].reshape(lanes, lanes))
    first_mix = fold_out(0, first_buf[:, depth + block :, :].reshape(lanes, lanes))
    drain(second_buf.at[pl.ds(0, chs - len(far))], parcel_recv.at[1])
    second_parts = parts_of(1, second_buf)
    last_gate = fold_in(1, last_gate_buf[...])
    last_mix = fold_out(
        1, dot_nt(second_buf[:, depth:, :].reshape(lanes, lanes), chosen).astype(BF16)
    )

    drain(block_buf, block_recv)
    values = jnp.concatenate(
        [block_buf[m * rows : (m + 1) * rows].reshape(n * n, block) for m in range(chs)], axis=1
    )
    pair = values.astype(F32)
    stats = statistics(pair)
    arms(values, stats, first_parts)
    gating = sigmoid(normed_product(dot_nt(values, first_gate[0]), stats, first_gate) + bias)
    right_k = [right_buf[pl.ds(k, n, stride=n), :] for k in range(n)]
    product = []
    for i in range(n):
        total = left_buf[i * n : i * n + 1, :] * right_k[0]
        for k in range(1, n):
            total = total + left_buf[i * n + k : i * n + k + 1, :] * right_k[k]
        product.append(total)
    mixed = mix(jnp.concatenate(product, axis=0), first_mix)
    values = (pair + gating * mixed).astype(BF16)
    middle = values.astype(F32)
    middle_buf[...] = middle

    arms(values, statistics(middle), second_parts)
    mine = middle_buf[pl.ds(pl.multiple_of(row * n, n), n), :]
    logits = normed_product(dot_nt(mine.astype(BF16), last_gate[0]), statistics(mine), last_gate)
    gating = sigmoid(logits + last_bias)
    kept = dot_nt(mine.astype(BF16), chosen)
    total = left_buf[pl.ds(row, 1), :] * right_buf[0:n, :]
    for k in range(1, n):
        total = total + left_buf[pl.ds(k * n + row, 1), :] * right_buf[k * n : (k + 1) * n, :]
    out_ref[...] = (kept + gating * mix(total, last_mix)).astype(BF16)

    drain(block_buf.at[pl.ds(0, rows * chs - 1)], block_send)
    drain(vector_buf.at[pl.ds(0, chs - 1)], vector_send)
    drain(first_buf.at[pl.ds(0, chs - 1)], weight_send.at[0])
    drain(second_buf.at[pl.ds(0, chs - 1)], weight_send.at[1])


def window_body(
    rows,
    chs,
    pair_rep,
    residue_mask,
    chain_ids,
    in_gain,
    in_bias,
    w_proj,
    w_gate,
    pair_bias,
    out_gain,
    out_bias,
    w_out,
):
    block, _, n = pair_rep.shape
    lanes = in_gain.shape[1]
    layers, _, parts, _ = w_proj.shape
    vmem = pl.BlockSpec(memory_space=pltpu.VMEM)
    hbm = pl.BlockSpec(memory_space=pl.ANY)
    dma = pltpu.SemaphoreType.DMA
    out = pl.pallas_call(
        functools.partial(window_kernel, rows, chs),
        out_shape=pltpu.VMEM((n, block), BF16),
        in_specs=[hbm] * 11,
        out_specs=vmem,
        scratch_shapes=[
            pltpu.SMEM(residue_mask.shape, jnp.int32),
            pltpu.SMEM(chain_ids.shape, jnp.int32),
            pltpu.VMEM((2, layers, lanes), F32),
            pltpu.VMEM((n, block), BF16),
            pltpu.VMEM((rows * chs, n, block), BF16),
            pltpu.VMEM((chs, (parts + 2) * block, lanes), BF16),
            pltpu.VMEM((chs, (parts + 1) * block, lanes), BF16),
            pltpu.VMEM((block, lanes), BF16),
            pltpu.VMEM((chs, 3, layers, block), F32),
            pltpu.VMEM((n * n, lanes), F32),
            pltpu.VMEM((n * n, lanes), F32),
            pltpu.VMEM((n * n, lanes), F32),
            pltpu.SemaphoreType.REGULAR,
            pltpu.SemaphoreType.REGULAR,
            dma((2,)),
            dma,
            dma,
            dma,
            dma,
            dma,
            dma((2,)),
            dma((3,)),
            dma((chs // 2 - 1, 3)),
            dma,
        ],
        compiler_params=pltpu.CompilerParams(collective_id=0, has_side_effects=True),
    )(
        residue_mask,
        chain_ids,
        jnp.swapaxes(pair_rep[:, 0, :], 0, 1),
        in_gain,
        in_bias,
        jnp.transpose(w_proj, (0, 2, 3, 1)).reshape(layers, parts * block, lanes),
        jnp.swapaxes(w_gate, 1, 2),
        pair_bias,
        out_gain,
        out_bias,
        w_out,
    )
    return jnp.swapaxes(out, 0, 1)[:, None, :]


def channel_norm(values, norm_gain, norm_bias):
    mean_val = jnp.mean(values, axis=0)
    variance = jnp.mean(values * values, axis=0) - mean_val * mean_val
    return (values - mean_val) * lax.rsqrt(variance + epsilon) * norm_gain[
        :, None, None
    ] + norm_bias[:, None, None]


def prepare(
    pair_local, layer, in_gain, in_bias, w_proj, w_gate, pair_bias, mask_rows, mask_cols, same_chain
):
    full_pair = lax.all_gather(pair_local, "ch", axis=0, tiled=True)
    normed = channel_norm(full_pair.astype(jnp.float32), in_gain[layer], in_bias[layer]).astype(
        jnp.bfloat16
    )
    projected = jnp.einsum(
        "cij,cpd->pdij", normed, w_proj[layer], preferred_element_type=jnp.float32
    )
    pair_mask = mask_rows[:, None] * mask_cols[None, :]
    first_arm = (jax.nn.sigmoid(projected[0]) * projected[1] * pair_mask).astype(jnp.bfloat16)
    second_arm = (jax.nn.sigmoid(projected[2]) * projected[3] * pair_mask).astype(jnp.bfloat16)
    logits = jnp.einsum("cij,cd->dij", normed, w_gate[layer], preferred_element_type=jnp.float32)
    logits = logits + pair_bias[layer][:, None, None] * same_chain[None]
    return (first_arm, second_arm, jax.nn.sigmoid(logits))


def finish(product_sum, gating, layer, out_gain, out_bias, w_out):
    totals = lax.psum(
        (jnp.sum(product_sum, axis=0), jnp.sum(product_sum * product_sum, axis=0)), "ch"
    )
    channels = product_sum.shape[0] * lax.axis_size("ch")
    mean_val = totals[0] / channels
    variance = totals[1] / channels - mean_val * mean_val
    scaled = (product_sum - mean_val) * lax.rsqrt(variance + epsilon)
    normed = (scaled * out_gain[layer][:, None, None] + out_bias[layer][:, None, None]).astype(
        jnp.bfloat16
    )
    columns = w_out[layer]
    mixed = lax.psum_scatter(
        jnp.einsum("dij,dc->cij", normed, columns, preferred_element_type=jnp.float32).astype(
            jnp.bfloat16
        ),
        "ch",
        scatter_dimension=0,
        tiled=True,
    ).astype(jnp.float32)
    return gating * mixed


def body(
    pair_rep,
    residue_mask,
    chain_ids,
    in_gain,
    in_bias,
    w_proj,
    w_gate,
    pair_bias,
    out_gain,
    out_bias,
    w_out,
):
    rows_here = pair_rep.shape[1]
    row_start = lax.axis_index("row") * rows_here
    mask_cols = residue_mask.astype(jnp.float32)
    mask_rows = lax.dynamic_slice_in_dim(mask_cols, row_start, rows_here)
    chain_rows = lax.dynamic_slice_in_dim(chain_ids, row_start, rows_here)
    same_chain = (chain_rows[:, None] == chain_ids[None, :]).astype(jnp.float32)
    first_arm, second_arm, gating = prepare(
        pair_rep, 0, in_gain, in_bias, w_proj, w_gate, pair_bias, mask_rows, mask_cols, same_chain
    )
    product_sum = jnp.einsum(
        "cik,cjk->cij",
        first_arm,
        lax.all_gather(second_arm, "row", axis=1, tiled=True),
        preferred_element_type=jnp.float32,
    )
    middle = (
        pair_rep.astype(jnp.float32) + finish(product_sum, gating, 0, out_gain, out_bias, w_out)
    ).astype(jnp.bfloat16)
    in_first, in_second, in_gating = prepare(
        middle, 1, in_gain, in_bias, w_proj, w_gate, pair_bias, mask_rows, mask_cols, same_chain
    )
    exchanged_left = lax.all_to_all(in_first, "row", split_axis=2, concat_axis=1, tiled=True)
    left_rows = jnp.swapaxes(exchanged_left, 1, 2)
    in_product = jnp.einsum(
        "cik,ckj->cij",
        left_rows,
        lax.all_gather(in_second, "row", axis=1, tiled=True),
        preferred_element_type=jnp.float32,
    )
    update = finish(in_product, in_gating, 1, out_gain, out_bias, w_out)
    return (middle.astype(jnp.float32) + update).astype(jnp.bfloat16)


def choose(rows, chs, *args):
    pair_rep, in_gain = args[0], args[3]
    n, lanes = pair_rep.shape[2], in_gain.shape[1]
    one_tile = pair_rep.shape[1] == 1 and n == rows == 8 and lanes == 128
    if one_tile and chs > 2 and chs % 2 == 0 and args[5].shape[1] == pair_rep.shape[0] * chs:
        return window_body(rows, chs, *args)
    return body(*args)


def solution(mesh):
    return jax.shard_map(
        functools.partial(choose, mesh.shape["row"], mesh.shape["ch"]),
        mesh=mesh,
        in_specs=(
            P("ch", "row", None),
            P(),
            P(),
            P(),
            P(),
            P(None, None, None, "ch"),
            P(None, None, "ch"),
            P(None, "ch"),
            P(None, "ch"),
            P(None, "ch"),
            P(None, "ch", None),
        ),
        out_specs=P("ch", "row", None),
        check_vma=False,
    )
```

```python
import functools
import jax
import jax.numpy as jnp
from jax import lax
from jax.experimental import pallas as pl
from jax.experimental.pallas import tpu as pltpu
from jax.sharding import PartitionSpec as P

epsilon = 1e-05
MESH = pl.DeviceIdType.MESH
F32 = jnp.float32
BF16 = jnp.bfloat16


def lane_norm(values, gain, bias):
    mean_val = jnp.mean(values, axis=-1, keepdims=True)
    variance = jnp.mean(values * values, axis=-1, keepdims=True) - mean_val * mean_val
    return ((values - mean_val) * lax.rsqrt(variance + epsilon) * gain + bias).astype(BF16)


def dot_nt(a, b):
    return lax.dot_general(a, b, (((1,), (1,)), ((), ())), preferred_element_type=F32)


def dot_nn(a, b):
    return lax.dot_general(a, b, (((1,), (0,)), ((), ())), preferred_element_type=F32)


def drain(ref, sem):
    pltpu.make_async_copy(ref, ref, sem).wait()


def window_kernel(
    rows,
    chs,
    mask_hbm,
    chain_hbm,
    pair_hbm,
    in_gain_hbm,
    in_bias_hbm,
    proj_hbm,
    gate_hbm,
    bias_hbm,
    gain_hbm,
    offset_hbm,
    mix_hbm,
    out_ref,
    mask_ref,
    chain_ref,
    norm_buf,
    own_buf,
    block_buf,
    first_buf,
    second_buf,
    last_gate_buf,
    vector_buf,
    left_buf,
    right_buf,
    middle_buf,
    near_sem,
    ready_sem,
    scalar_sem,
    norm_sem,
    own_sem,
    block_send,
    block_recv,
    vector_send,
    weight_send,
    parcel_recv,
    far_recv,
    gate_sem,
):
    n = out_ref.shape[0]
    lanes = norm_buf.shape[2]
    block = lanes // chs
    depth = proj_hbm.shape[1]
    row = lax.axis_index("row")
    ch = lax.axis_index("ch")
    here = row * chs + ch

    last = rows - 1
    cores = 2
    partner = ch + 1 - 2 * lax.rem(ch, cores)
    far = [lax.rem(ch + cores * step, chs) for step in range(1, chs // cores)]
    mates = far + [partner]
    is_last = here == rows * chs - 1

    barrier = pltpu.get_barrier_semaphore()

    def greet(r, c):
        pl.semaphore_signal(barrier, inc=1, device_id=(r, c), device_id_type=MESH)

    @pl.when(jnp.logical_not(is_last))
    def _():
        greet(last, chs - 1)

    @pl.when(here < cores)
    def _():
        for m in reversed(range(chs - 1)):
            greet(last, m)

        @pl.loop(1, last)
        def _(back):
            for m in range(chs):
                greet(last - back, m)

        @pl.loop(ch + 1, chs)
        def _(other):
            greet(0, other)

    for mate in mates:

        @pl.when((mate > ch) & (row < last) & (here >= cores))
        def _():
            greet(row, mate)

    lower_mates = lax.rem(ch, cores) + ch // cores
    greeted_above = jnp.minimum(ch, cores) + jnp.where(ch < cores, 0, lower_mates - 1)
    greetings = jnp.where(
        row == 0,
        greeted_above,
        jnp.where(row < last, cores + lower_mates, jnp.where(is_last, rows * chs - 1, cores)),
    )

    def send(src, dst, send_sem, recv_sem, r, c):
        pltpu.make_async_remote_copy(
            src_ref=src,
            dst_ref=dst,
            send_sem=send_sem,
            recv_sem=recv_sem,
            device_id=(r, c),
            device_id_type=MESH,
        ).start()

    def send_block(src, r, c):
        send(src, block_buf.at[ch * rows + row], block_send, block_recv, r, c)

    @pl.when(here > 0)
    def _():
        pl.semaphore_wait(barrier, greetings)

    for m in range(cores):

        @pl.when(here > m)
        def _():
            send_block(pair_hbm, 0, m)

    @pl.when(is_last)
    def _():
        @pl.loop(0, last)
        def _(other):
            for m in range(chs):
                pl.semaphore_signal(ready_sem, inc=1, device_id=(other, m), device_id_type=MESH)

        for m in range(chs - 1):
            pl.semaphore_signal(ready_sem, inc=1, device_id=(last, m), device_id_type=MESH)

    for mate in mates:

        @pl.when((mate < ch) & (row < last))
        def _():
            pl.semaphore_signal(near_sem, inc=1, device_id=(row, mate), device_id_type=MESH)

    pltpu.make_async_copy(pair_hbm, own_buf, own_sem).start()
    pltpu.make_async_copy(pair_hbm, block_buf.at[ch * rows + row], block_recv).start()
    vectors = [
        (ref, vector_buf.at[ch, t], vector_send, 2)
        for t, ref in enumerate((bias_hbm, gain_hbm, offset_hbm))
    ]
    pieces = (
        (0, proj_hbm, first_buf, 0, depth),
        (0, gate_hbm, first_buf, depth, block),
        (0, mix_hbm, first_buf, depth + block, block),
        (1, proj_hbm, second_buf, 0, depth),
        (1, mix_hbm, second_buf, depth, block),
    )
    weights = [
        (ref.at[u], buf.at[ch, pl.ds(at, size)], weight_send.at[u], u)
        for u, ref, buf, at, size in pieces
    ]
    parcels = weights[:3] + vectors + weights[3:]
    for src, dst, _, k in parcels:
        pltpu.make_async_copy(src, dst, parcel_recv.at[k]).start()
    pltpu.make_async_copy(mask_hbm, mask_ref, scalar_sem.at[0]).start()
    pltpu.make_async_copy(chain_hbm, chain_ref, scalar_sem.at[1]).start()
    pltpu.make_async_copy(in_gain_hbm, norm_buf.at[0], norm_sem).start()
    pltpu.make_async_copy(in_bias_hbm, norm_buf.at[1], norm_sem).start()
    pltpu.make_async_copy(gate_hbm.at[1], last_gate_buf, gate_sem).start()

    def give(step):
        for src, dst, send_sem, k in parcels:
            recv_sem = far_recv.at[step, k] if step < len(far) else parcel_recv.at[k]
            send(src, dst, send_sem, recv_sem, row, mates[step])

    for step, mate in enumerate(mates):

        @pl.when((mate < ch) & (row < last))
        def _():
            give(step)

    @pl.when((row < last) & (ch < chs - 1))
    def _():
        pl.semaphore_wait(near_sem, len(mates) - lower_mates)

    @pl.when((row == last) & jnp.logical_not(is_last))
    def _():
        pl.semaphore_wait(ready_sem, 1)

    for step, mate in enumerate(mates):

        @pl.when((mate > ch) | (row == last))
        def _():
            give(step)

    def pass_on():
        for k, buf, send_sem in (
            (0, first_buf, weight_send.at[0]),
            (2, vector_buf, vector_send),
            (1, second_buf, weight_send.at[1]),
        ):
            for step in range(len(far)):
                piece = buf.at[lax.rem(ch + chs - cores * (step + 1), chs)]
                drain(piece, far_recv.at[step, k])
                send(piece, piece, send_sem, parcel_recv.at[k], row, partner)

    drain(own_buf, own_sem)

    @pl.when(here < cores)
    def _():
        pass_on()

    @pl.when(row < last)
    def _():
        pl.semaphore_wait(ready_sem, 1)

    for m in reversed(range(1, chs)):

        @pl.when(here < m if m < cores else (here != m))
        def _():
            send_block(own_buf, 0, m)

    @pl.when(row > 0)
    def _():
        for step in range(1, chs):
            send_block(own_buf, row, lax.rem(ch + step, chs))

    @pl.loop(1, row)
    def _(other):
        for m in reversed(range(chs)):
            send_block(own_buf, other, m)

    @pl.loop(row + 1, rows)
    def _(other):
        for m in reversed(range(chs)):
            send_block(own_buf, other, m)

    @pl.when(here >= cores)
    def _():
        pass_on()

    drain(mask_hbm, scalar_sem.at[0])
    drain(chain_hbm, scalar_sem.at[1])
    place = lax.broadcasted_iota(jnp.int32, (n, lanes), 0)
    mask_j = jnp.zeros((n, lanes), jnp.int32)
    chain_j = jnp.zeros((n, lanes), jnp.int32)
    for j in range(n):
        mask_j = jnp.where(place == j, mask_ref[j], mask_j)
        chain_j = jnp.where(place == j, chain_ref[j], chain_j)
    pair_mask = jnp.concatenate([(mask_j * mask_ref[i]).astype(F32) for i in range(n)], axis=0)
    same_chain = jnp.concatenate(
        [jnp.where(chain_j == chain_ref[i], 1.0, 0.0).astype(F32) for i in range(n)], axis=0
    )
    same_here = jnp.where(chain_j == chain_ref[row], 1.0, 0.0).astype(F32)

    def vector(t, u):
        return jnp.concatenate([vector_buf[m, t, u : u + 1, :] for m in range(chs)], axis=1)

    drain(norm_buf, norm_sem)
    drain(vector_buf.at[pl.ds(0, chs - len(far))], parcel_recv.at[2])
    bias = (0.5 * vector(0, 0)) * same_chain
    gains = [vector(1, u) for u in range(2)]
    offsets = [vector(2, u) for u in range(2)]
    last_bias = (0.5 * vector_buf[ch, 0, 1:2, :]) * same_here[:, 0:block]

    picked = lax.broadcasted_iota(jnp.int32, (block, lanes), 1)
    wanted = lax.broadcasted_iota(jnp.int32, (block, lanes), 0) + ch * block
    chosen = jnp.where(picked == wanted, 1.0, 0.0).astype(BF16)
    diagonal = lax.broadcasted_iota(jnp.int32, (lanes, lanes), 0) == lax.broadcasted_iota(
        jnp.int32, (lanes, lanes), 1
    )
    def halves(values):
        high = values.astype(BF16)
        return high, (values - high.astype(F32)).astype(BF16)

    def tail_of(*rows_of):
        count = 2 * n
        place_of = lax.broadcasted_iota(jnp.int32, (count, rows_of[0].shape[1]), 0)
        tail = jnp.zeros(place_of.shape, F32)
        for i, values in enumerate(rows_of):
            tail = jnp.where(place_of == i, values.astype(F32), tail)
        return tail.astype(BF16)

    one = jnp.ones((1, lanes), F32)
    in_tails, out_tails = [], []
    for u in range(2):
        ratio = norm_buf[1, u : u + 1, :] / norm_buf[0, u : u + 1, :]
        in_tails.append(tail_of(one, *halves(ratio)))
        out_tails.append(tail_of(one, *halves(offsets[u] / gains[u])))

    def statistics(values):
        mean_val = jnp.mean(values, axis=-1, keepdims=True)
        variance = jnp.mean(values * values, axis=-1, keepdims=True) - mean_val * mean_val
        scale = lax.rsqrt(variance + epsilon)
        return scale, scale * mean_val

    def gate_of(values):
        return jnp.tanh(values) + 1.0

    def fold(dot, scaled, tail):
        product = dot(tail, scaled)
        return scaled, product[0:1], product[1:2] + product[2:3]

    def normed_product(product, stats, folded):
        return product * stats[0] + (folded[2] - stats[1] * folded[1])

    def fold_in(u, weight):
        scaled = (weight.astype(F32) * (0.5 * norm_buf[0, u : u + 1, :])).astype(BF16)
        return fold(dot_nt, scaled, in_tails[u])

    def fold_out(u, weight):
        column = jnp.sum(jnp.where(diagonal, gains[u], 0.0), axis=-1, keepdims=True)
        scaled = (weight.astype(F32) * (0.5 * column)).astype(BF16)
        return fold(dot_nn, scaled, out_tails[u])

    def parts_of(u, buf):
        weights = [
            buf[:, part * block : (part + 1) * block, :].reshape(lanes, lanes)
            for part in range(depth // block)
        ]
        return [
            fold_in(u, jnp.concatenate(weights[first : first + 4], axis=0))
            for first in range(0, len(weights), 4)
        ]

    def arms(values, stats, folded):
        value = [normed_product(dot_nt(values, part[0]), stats, part) for part in folded]
        value = [
            wide[:, first : first + lanes]
            for wide in value
            for first in range(0, wide.shape[1], lanes)
        ]
        left_buf[...] = gate_of(value[0]) * (value[1] * pair_mask)
        right_buf[...] = gate_of(value[2]) * (value[3] * pair_mask)

    def mix(values, folded):
        both = jnp.concatenate(halves(values), axis=1)
        product = dot_nn(both, jnp.concatenate([folded[0], folded[0]], axis=0))
        return normed_product(product, statistics(values), folded)

    drain(last_gate_buf, gate_sem)
    drain(first_buf.at[pl.ds(0, chs - len(far))], parcel_recv.at[0])
    first_parts = parts_of(0, first_buf)
    first_gate = fold_in(0, first_buf[:, depth : depth + block, :].reshape(lanes, lanes))
    first_mix = fold_out(0, first_buf[:, depth + block :, :].reshape(lanes, lanes))
    drain(second_buf.at[pl.ds(0, chs - len(far))], parcel_recv.at[1])
    second_parts = parts_of(1, second_buf)
    last_gate = fold_in(1, last_gate_buf[...])
    last_mix = fold_out(
        1, dot_nt(second_buf[:, depth:, :].reshape(lanes, lanes), chosen).astype(BF16)
    )

    drain(block_buf, block_recv)
    values = jnp.concatenate(
        [block_buf[m * rows : (m + 1) * rows].reshape(n * n, block) for m in range(chs)], axis=1
    )
    pair = values.astype(F32)
    stats = statistics(pair)
    arms(values, stats, first_parts)
    gating = gate_of(normed_product(dot_nt(values, first_gate[0]), stats, first_gate) + bias)
    right_k = [right_buf[pl.ds(k, n, stride=n), :] for k in range(n)]
    product = []
    for i in range(n):
        total = left_buf[i * n : i * n + 1, :] * right_k[0]
        for k in range(1, n):
            total = total + left_buf[i * n + k : i * n + k + 1, :] * right_k[k]
        product.append(total)
    mixed = mix(jnp.concatenate(product, axis=0), first_mix)
    values = (pair + gating * mixed).astype(BF16)
    middle = values.astype(F32)
    middle_buf[...] = middle

    arms(values, statistics(middle), second_parts)
    mine = middle_buf[pl.ds(pl.multiple_of(row * n, n), n), :]
    logits = normed_product(dot_nt(mine.astype(BF16), last_gate[0]), statistics(mine), last_gate)
    gating = gate_of(logits + last_bias)
    kept = dot_nt(mine.astype(BF16), chosen)
    total = left_buf[pl.ds(row, 1), :] * right_buf[0:n, :]
    for k in range(1, n):
        total = total + left_buf[pl.ds(k * n + row, 1), :] * right_buf[k * n : (k + 1) * n, :]
    out_ref[...] = (kept + gating * mix(total, last_mix)).astype(BF16)

    drain(block_buf.at[pl.ds(0, rows * chs - 1)], block_send)
    drain(vector_buf.at[pl.ds(0, chs - 1)], vector_send)
    drain(first_buf.at[pl.ds(0, chs - 1)], weight_send.at[0])
    drain(second_buf.at[pl.ds(0, chs - 1)], weight_send.at[1])


def window_body(
    rows,
    chs,
    pair_rep,
    residue_mask,
    chain_ids,
    in_gain,
    in_bias,
    w_proj,
    w_gate,
    pair_bias,
    out_gain,
    out_bias,
    w_out,
):
    block, _, n = pair_rep.shape
    lanes = in_gain.shape[1]
    layers, _, parts, _ = w_proj.shape
    vmem = pl.BlockSpec(memory_space=pltpu.VMEM)
    hbm = pl.BlockSpec(memory_space=pl.ANY)
    dma = pltpu.SemaphoreType.DMA
    out = pl.pallas_call(
        functools.partial(window_kernel, rows, chs),
        out_shape=pltpu.VMEM((n, block), BF16),
        in_specs=[hbm] * 11,
        out_specs=vmem,
        scratch_shapes=[
            pltpu.SMEM(residue_mask.shape, jnp.int32),
            pltpu.SMEM(chain_ids.shape, jnp.int32),
            pltpu.VMEM((2, layers, lanes), F32),
            pltpu.VMEM((n, block), BF16),
            pltpu.VMEM((rows * chs, n, block), BF16),
            pltpu.VMEM((chs, (parts + 2) * block, lanes), BF16),
            pltpu.VMEM((chs, (parts + 1) * block, lanes), BF16),
            pltpu.VMEM((block, lanes), BF16),
            pltpu.VMEM((chs, 3, layers, block), F32),
            pltpu.VMEM((n * n, lanes), F32),
            pltpu.VMEM((n * n, lanes), F32),
            pltpu.VMEM((n * n, lanes), F32),
            pltpu.SemaphoreType.REGULAR,
            pltpu.SemaphoreType.REGULAR,
            dma((2,)),
            dma,
            dma,
            dma,
            dma,
            dma,
            dma((2,)),
            dma((3,)),
            dma((chs // 2 - 1, 3)),
            dma,
        ],
        compiler_params=pltpu.CompilerParams(collective_id=0, has_side_effects=True),
    )(
        residue_mask,
        chain_ids,
        jnp.swapaxes(pair_rep[:, 0, :], 0, 1),
        in_gain,
        in_bias,
        jnp.transpose(w_proj, (0, 2, 3, 1)).reshape(layers, parts * block, lanes),
        jnp.swapaxes(w_gate, 1, 2),
        pair_bias,
        out_gain,
        out_bias,
        w_out,
    )
    return jnp.swapaxes(out, 0, 1)[:, None, :]


def channel_norm(values, norm_gain, norm_bias):
    mean_val = jnp.mean(values, axis=0)
    variance = jnp.mean(values * values, axis=0) - mean_val * mean_val
    return (values - mean_val) * lax.rsqrt(variance + epsilon) * norm_gain[
        :, None, None
    ] + norm_bias[:, None, None]


def prepare(
    pair_local, layer, in_gain, in_bias, w_proj, w_gate, pair_bias, mask_rows, mask_cols, same_chain
):
    full_pair = lax.all_gather(pair_local, "ch", axis=0, tiled=True)
    normed = channel_norm(full_pair.astype(jnp.float32), in_gain[layer], in_bias[layer]).astype(
        jnp.bfloat16
    )
    projected = jnp.einsum(
        "cij,cpd->pdij", normed, w_proj[layer], preferred_element_type=jnp.float32
    )
    pair_mask = mask_rows[:, None] * mask_cols[None, :]
    first_arm = (jax.nn.sigmoid(projected[0]) * projected[1] * pair_mask).astype(jnp.bfloat16)
    second_arm = (jax.nn.sigmoid(projected[2]) * projected[3] * pair_mask).astype(jnp.bfloat16)
    logits = jnp.einsum("cij,cd->dij", normed, w_gate[layer], preferred_element_type=jnp.float32)
    logits = logits + pair_bias[layer][:, None, None] * same_chain[None]
    return (first_arm, second_arm, jax.nn.sigmoid(logits))


def finish(product_sum, gating, layer, out_gain, out_bias, w_out):
    totals = lax.psum(
        (jnp.sum(product_sum, axis=0), jnp.sum(product_sum * product_sum, axis=0)), "ch"
    )
    channels = product_sum.shape[0] * lax.axis_size("ch")
    mean_val = totals[0] / channels
    variance = totals[1] / channels - mean_val * mean_val
    scaled = (product_sum - mean_val) * lax.rsqrt(variance + epsilon)
    normed = (scaled * out_gain[layer][:, None, None] + out_bias[layer][:, None, None]).astype(
        jnp.bfloat16
    )
    columns = w_out[layer]
    mixed = lax.psum_scatter(
        jnp.einsum("dij,dc->cij", normed, columns, preferred_element_type=jnp.float32).astype(
            jnp.bfloat16
        ),
        "ch",
        scatter_dimension=0,
        tiled=True,
    ).astype(jnp.float32)
    return gating * mixed


def body(
    pair_rep,
    residue_mask,
    chain_ids,
    in_gain,
    in_bias,
    w_proj,
    w_gate,
    pair_bias,
    out_gain,
    out_bias,
    w_out,
):
    rows_here = pair_rep.shape[1]
    row_start = lax.axis_index("row") * rows_here
    mask_cols = residue_mask.astype(jnp.float32)
    mask_rows = lax.dynamic_slice_in_dim(mask_cols, row_start, rows_here)
    chain_rows = lax.dynamic_slice_in_dim(chain_ids, row_start, rows_here)
    same_chain = (chain_rows[:, None] == chain_ids[None, :]).astype(jnp.float32)
    first_arm, second_arm, gating = prepare(
        pair_rep, 0, in_gain, in_bias, w_proj, w_gate, pair_bias, mask_rows, mask_cols, same_chain
    )
    product_sum = jnp.einsum(
        "cik,cjk->cij",
        first_arm,
        lax.all_gather(second_arm, "row", axis=1, tiled=True),
        preferred_element_type=jnp.float32,
    )
    middle = (
        pair_rep.astype(jnp.float32) + finish(product_sum, gating, 0, out_gain, out_bias, w_out)
    ).astype(jnp.bfloat16)
    in_first, in_second, in_gating = prepare(
        middle, 1, in_gain, in_bias, w_proj, w_gate, pair_bias, mask_rows, mask_cols, same_chain
    )
    exchanged_left = lax.all_to_all(in_first, "row", split_axis=2, concat_axis=1, tiled=True)
    left_rows = jnp.swapaxes(exchanged_left, 1, 2)
    in_product = jnp.einsum(
        "cik,ckj->cij",
        left_rows,
        lax.all_gather(in_second, "row", axis=1, tiled=True),
        preferred_element_type=jnp.float32,
    )
    update = finish(in_product, in_gating, 1, out_gain, out_bias, w_out)
    return (middle.astype(jnp.float32) + update).astype(jnp.bfloat16)


def choose(rows, chs, *args):
    pair_rep, in_gain = args[0], args[3]
    n, lanes = pair_rep.shape[2], in_gain.shape[1]
    one_tile = pair_rep.shape[1] == 1 and n == rows == 8 and lanes == 128
    if one_tile and chs > 2 and chs % 2 == 0 and args[5].shape[1] == pair_rep.shape[0] * chs:
        return window_body(rows, chs, *args)
    return body(*args)


def solution(mesh):
    return jax.shard_map(
        functools.partial(choose, mesh.shape["row"], mesh.shape["ch"]),
        mesh=mesh,
        in_specs=(
            P("ch", "row", None),
            P(),
            P(),
            P(),
            P(),
            P(None, None, None, "ch"),
            P(None, None, "ch"),
            P(None, "ch"),
            P(None, "ch"),
            P(None, "ch"),
            P(None, "ch", None),
        ),
        out_specs=P("ch", "row", None),
        check_vma=False,
    )
```

```python
import functools
import jax
import jax.numpy as jnp
from jax import lax
from jax.experimental import pallas as pl
from jax.experimental.pallas import tpu as pltpu
from jax.sharding import PartitionSpec as P

epsilon = 1e-05
MESH = pl.DeviceIdType.MESH
F32 = jnp.float32
BF16 = jnp.bfloat16


def lane_norm(values, gain, bias):
    mean_val = jnp.mean(values, axis=-1, keepdims=True)
    variance = jnp.mean(values * values, axis=-1, keepdims=True) - mean_val * mean_val
    return ((values - mean_val) * lax.rsqrt(variance + epsilon) * gain + bias).astype(BF16)


def dot_nt(a, b):
    return lax.dot_general(a, b, (((1,), (1,)), ((), ())), preferred_element_type=F32)


def dot_nn(a, b):
    return lax.dot_general(a, b, (((1,), (0,)), ((), ())), preferred_element_type=F32)


def drain(ref, sem):
    pltpu.make_async_copy(ref, ref, sem).wait()


def window_kernel(
    rows,
    chs,
    mask_hbm,
    chain_hbm,
    pair_hbm,
    in_gain_hbm,
    in_bias_hbm,
    proj_hbm,
    gate_hbm,
    bias_hbm,
    gain_hbm,
    offset_hbm,
    mix_hbm,
    out_ref,
    mask_ref,
    chain_ref,
    norm_buf,
    own_buf,
    block_buf,
    weight_buf,
    last_gate_buf,
    vector_buf,
    left_buf,
    right_buf,
    middle_buf,
    near_sem,
    ready_sem,
    scalar_sem,
    norm_sem,
    own_sem,
    block_send,
    block_recv,
    vector_send,
    weight_send,
    parcel_recv,
    far_recv,
    gate_sem,
):
    n = out_ref.shape[0]
    lanes = norm_buf.shape[2]
    block = lanes // chs
    depth = proj_hbm.shape[1]
    split = depth + 2 * block
    row = lax.axis_index("row")
    ch = lax.axis_index("ch")
    here = row * chs + ch

    last = rows - 1
    cores = 2
    partner = ch + 1 - 2 * lax.rem(ch, cores)
    far = [lax.rem(ch + cores * step, chs) for step in range(1, chs // cores)]
    mates = far + [partner]
    is_last = here == rows * chs - 1

    barrier = pltpu.get_barrier_semaphore()

    def greet(r, c):
        pl.semaphore_signal(barrier, inc=1, device_id=(r, c), device_id_type=MESH)

    @pl.when(jnp.logical_not(is_last))
    def _():
        greet(last, chs - 1)

    @pl.when(here < cores)
    def _():
        for m in reversed(range(chs - 1)):
            greet(last, m)

        @pl.loop(1, last)
        def _(back):
            for m in range(chs):
                greet(last - back, m)

        @pl.loop(ch + 1, chs)
        def _(other):
            greet(0, other)

    for mate in mates:

        @pl.when((mate > ch) & (row < last) & (here >= cores))
        def _():
            greet(row, mate)

    lower_mates = lax.rem(ch, cores) + ch // cores
    greeted_above = jnp.minimum(ch, cores) + jnp.where(ch < cores, 0, lower_mates - 1)
    greetings = jnp.where(
        row == 0,
        greeted_above,
        jnp.where(row < last, cores + lower_mates, jnp.where(is_last, rows * chs - 1, cores)),
    )

    def send(src, dst, send_sem, recv_sem, r, c):
        pltpu.make_async_remote_copy(
            src_ref=src,
            dst_ref=dst,
            send_sem=send_sem,
            recv_sem=recv_sem,
            device_id=(r, c),
            device_id_type=MESH,
        ).start()

    def send_block(src, r, c):
        send(src, block_buf.at[ch * rows + row], block_send, block_recv, r, c)

    @pl.when(here > 0)
    def _():
        pl.semaphore_wait(barrier, greetings)

    for m in range(cores):

        @pl.when(here > m)
        def _():
            send_block(pair_hbm, 0, m)

    @pl.when(is_last)
    def _():
        @pl.loop(0, last)
        def _(other):
            for m in range(chs):
                pl.semaphore_signal(ready_sem, inc=1, device_id=(other, m), device_id_type=MESH)

        for m in range(chs - 1):
            pl.semaphore_signal(ready_sem, inc=1, device_id=(last, m), device_id_type=MESH)

    for mate in mates:

        @pl.when((mate < ch) & (row < last))
        def _():
            pl.semaphore_signal(near_sem, inc=1, device_id=(row, mate), device_id_type=MESH)

    pltpu.make_async_copy(pair_hbm, own_buf, own_sem).start()
    pltpu.make_async_copy(pair_hbm, block_buf.at[ch * rows + row], block_recv).start()
    vectors = [
        (ref, vector_buf.at[ch, t], vector_send, 2)
        for t, ref in enumerate((bias_hbm, gain_hbm, offset_hbm))
    ]
    pieces = (
        (0, proj_hbm, weight_buf, 0, depth),
        (0, gate_hbm, weight_buf, depth, block),
        (0, mix_hbm, weight_buf, depth + block, block),
        (1, proj_hbm, weight_buf, split, depth),
        (1, mix_hbm, weight_buf, split + depth, block),
    )
    weights = [
        (ref.at[u], buf.at[ch, pl.ds(at, size)], weight_send, u)
        for u, ref, buf, at, size in pieces
    ]
    parcels = weights[:3] + vectors + weights[3:]
    for src, dst, _, k in parcels:
        pltpu.make_async_copy(src, dst, parcel_recv.at[k]).start()
    pltpu.make_async_copy(mask_hbm, mask_ref, scalar_sem.at[0]).start()
    pltpu.make_async_copy(chain_hbm, chain_ref, scalar_sem.at[1]).start()
    pltpu.make_async_copy(in_gain_hbm, norm_buf.at[0], norm_sem).start()
    pltpu.make_async_copy(in_bias_hbm, norm_buf.at[1], norm_sem).start()
    pltpu.make_async_copy(gate_hbm.at[1], last_gate_buf, gate_sem).start()

    def give(step):
        for src, dst, send_sem, k in parcels:
            recv_sem = far_recv.at[step, k] if step < len(far) else parcel_recv.at[k]
            send(src, dst, send_sem, recv_sem, row, mates[step])

    for step, mate in enumerate(mates):

        @pl.when((mate < ch) & (row < last))
        def _():
            give(step)

    @pl.when((row < last) & (ch < chs - 1))
    def _():
        pl.semaphore_wait(near_sem, len(mates) - lower_mates)

    @pl.when((row == last) & jnp.logical_not(is_last))
    def _():
        pl.semaphore_wait(ready_sem, 1)

    for step, mate in enumerate(mates):

        @pl.when((mate > ch) | (row == last))
        def _():
            give(step)

    def pass_on():
        for k, buf, send_sem in (
            (0, weight_buf.at[:, pl.ds(0, split)], weight_send),
            (2, vector_buf, vector_send),
            (1, weight_buf.at[:, pl.ds(split, depth + block)], weight_send),
        ):
            for step in range(len(far)):
                piece = buf.at[lax.rem(ch + chs - cores * (step + 1), chs)]
                drain(piece, far_recv.at[step, k])
                send(piece, piece, send_sem, parcel_recv.at[k], row, partner)

    drain(own_buf, own_sem)

    @pl.when(here < cores)
    def _():
        pass_on()

    @pl.when(row < last)
    def _():
        pl.semaphore_wait(ready_sem, 1)

    for m in reversed(range(1, chs)):

        @pl.when(here < m if m < cores else (here != m))
        def _():
            send_block(own_buf, 0, m)

    @pl.when(row > 0)
    def _():
        for step in range(1, chs):
            send_block(own_buf, row, lax.rem(ch + step, chs))

    @pl.loop(1, row)
    def _(other):
        for m in reversed(range(chs)):
            send_block(own_buf, other, m)

    @pl.loop(row + 1, rows)
    def _(other):
        for m in reversed(range(chs)):
            send_block(own_buf, other, m)

    @pl.when(here >= cores)
    def _():
        pass_on()

    drain(mask_hbm, scalar_sem.at[0])
    drain(chain_hbm, scalar_sem.at[1])
    place = lax.broadcasted_iota(jnp.int32, (n, lanes), 0)
    mask_j = jnp.zeros((n, lanes), jnp.int32)
    chain_j = jnp.zeros((n, lanes), jnp.int32)
    for j in range(n):
        mask_j = jnp.where(place == j, mask_ref[j], mask_j)
        chain_j = jnp.where(place == j, chain_ref[j], chain_j)
    pair_mask = jnp.concatenate([(mask_j * mask_ref[i]).astype(F32) for i in range(n)], axis=0)
    same_chain = jnp.concatenate(
        [jnp.where(chain_j == chain_ref[i], 1.0, 0.0).astype(F32) for i in range(n)], axis=0
    )
    same_here = jnp.where(chain_j == chain_ref[row], 1.0, 0.0).astype(F32)

    def vector(t, u):
        return jnp.concatenate([vector_buf[m, t, u : u + 1, :] for m in range(chs)], axis=1)

    drain(norm_buf, norm_sem)
    drain(vector_buf.at[pl.ds(0, chs - len(far))], parcel_recv.at[2])
    bias = (0.5 * vector(0, 0)) * same_chain
    gains = [vector(1, u) for u in range(2)]
    offsets = [vector(2, u) for u in range(2)]
    last_bias = (0.5 * vector_buf[ch, 0, 1:2, :]) * same_here[:, 0:block]

    picked = lax.broadcasted_iota(jnp.int32, (block, lanes), 1)
    wanted = lax.broadcasted_iota(jnp.int32, (block, lanes), 0) + ch * block
    chosen = jnp.where(picked == wanted, 1.0, 0.0).astype(BF16)
    diagonal = lax.broadcasted_iota(jnp.int32, (lanes, lanes), 0) == lax.broadcasted_iota(
        jnp.int32, (lanes, lanes), 1
    )
    def halves(values):
        high = values.astype(BF16)
        return high, (values - high.astype(F32)).astype(BF16)

    def tail_of(*rows_of):
        count = 2 * n
        place_of = lax.broadcasted_iota(jnp.int32, (count, rows_of[0].shape[1]), 0)
        tail = jnp.zeros(place_of.shape, F32)
        for i, values in enumerate(rows_of):
            tail = jnp.where(place_of == i, values.astype(F32), tail)
        return tail.astype(BF16)

    one = jnp.ones((1, lanes), F32)
    in_tails, out_tails = [], []
    for u in range(2):
        ratio = norm_buf[1, u : u + 1, :] / norm_buf[0, u : u + 1, :]
        in_tails.append(tail_of(one, *halves(ratio)))
        out_tails.append(tail_of(one, *halves(offsets[u] / gains[u])))

    def statistics(values):
        mean_val = jnp.mean(values, axis=-1, keepdims=True)
        variance = jnp.mean(values * values, axis=-1, keepdims=True) - mean_val * mean_val
        scale = lax.rsqrt(variance + epsilon)
        return scale, scale * mean_val

    def gate_of(values):
        return jnp.tanh(values) + 1.0

    def fold(dot, scaled, tail):
        product = dot(tail, scaled)
        return scaled, product[0:1], product[1:2] + product[2:3]

    def normed_product(product, stats, folded):
        return product * stats[0] + (folded[2] - stats[1] * folded[1])

    def fold_in(u, weight):
        scaled = (weight.astype(F32) * (0.5 * norm_buf[0, u : u + 1, :])).astype(BF16)
        return fold(dot_nt, scaled, in_tails[u])

    def fold_out(u, weight):
        column = jnp.sum(jnp.where(diagonal, gains[u], 0.0), axis=-1, keepdims=True)
        scaled = (weight.astype(F32) * (0.5 * column)).astype(BF16)
        return fold(dot_nn, scaled, out_tails[u])

    def parts_of(u, buf, at):
        weights = [
            buf[:, at + part * block : at + (part + 1) * block, :].reshape(lanes, lanes)
            for part in range(depth // block)
        ]
        return [
            fold_in(u, jnp.concatenate(weights[first : first + 4], axis=0))
            for first in range(0, len(weights), 4)
        ]

    def arms(values, stats, folded):
        value = [normed_product(dot_nt(values, part[0]), stats, part) for part in folded]
        value = [
            wide[:, first : first + lanes]
            for wide in value
            for first in range(0, wide.shape[1], lanes)
        ]
        left_buf[...] = gate_of(value[0]) * (value[1] * pair_mask)
        right_buf[...] = gate_of(value[2]) * (value[3] * pair_mask)

    def mix(values, folded):
        both = jnp.concatenate(halves(values), axis=1)
        product = dot_nn(both, jnp.concatenate([folded[0], folded[0]], axis=0))
        return normed_product(product, statistics(values), folded)

    drain(last_gate_buf, gate_sem)
    drain(weight_buf.at[pl.ds(0, chs - len(far)), pl.ds(0, split)], parcel_recv.at[0])
    first_parts = parts_of(0, weight_buf, 0)
    first_gate = fold_in(0, weight_buf[:, depth : depth + block, :].reshape(lanes, lanes))
    first_mix = fold_out(0, weight_buf[:, depth + block : split, :].reshape(lanes, lanes))
    drain(weight_buf.at[pl.ds(0, chs - len(far)), pl.ds(split, depth + block)], parcel_recv.at[1])
    second_parts = parts_of(1, weight_buf, split)
    last_gate = fold_in(1, last_gate_buf[...])
    last_mix = fold_out(
        1, dot_nt(weight_buf[:, split + depth :, :].reshape(lanes, lanes), chosen).astype(BF16)
    )

    drain(block_buf, block_recv)
    values = jnp.concatenate(
        [block_buf[m * rows : (m + 1) * rows].reshape(n * n, block) for m in range(chs)], axis=1
    )
    pair = values.astype(F32)
    stats = statistics(pair)
    arms(values, stats, first_parts)
    gating = gate_of(normed_product(dot_nt(values, first_gate[0]), stats, first_gate) + bias)
    right_k = [right_buf[pl.ds(k, n, stride=n), :] for k in range(n)]
    product = []
    for i in range(n):
        total = left_buf[i * n : i * n + 1, :] * right_k[0]
        for k in range(1, n):
            total = total + left_buf[i * n + k : i * n + k + 1, :] * right_k[k]
        product.append(total)
    mixed = mix(jnp.concatenate(product, axis=0), first_mix)
    values = (pair + gating * mixed).astype(BF16)
    middle = values.astype(F32)
    middle_buf[...] = middle

    arms(values, statistics(middle), second_parts)
    mine = middle_buf[pl.ds(pl.multiple_of(row * n, n), n), :]
    logits = normed_product(dot_nt(mine.astype(BF16), last_gate[0]), statistics(mine), last_gate)
    gating = gate_of(logits + last_bias)
    kept = dot_nt(mine.astype(BF16), chosen)
    total = left_buf[pl.ds(row, 1), :] * right_buf[0:n, :]
    for k in range(1, n):
        total = total + left_buf[pl.ds(k * n + row, 1), :] * right_buf[k * n : (k + 1) * n, :]
    out_ref[...] = (kept + gating * mix(total, last_mix)).astype(BF16)

    drain(block_buf.at[pl.ds(0, rows * chs - 1)], block_send)
    drain(vector_buf.at[pl.ds(0, chs - 1)], vector_send)
    drain(weight_buf.at[pl.ds(0, chs - 1)], weight_send)


def window_body(
    rows,
    chs,
    pair_rep,
    residue_mask,
    chain_ids,
    in_gain,
    in_bias,
    w_proj,
    w_gate,
    pair_bias,
    out_gain,
    out_bias,
    w_out,
):
    block, _, n = pair_rep.shape
    lanes = in_gain.shape[1]
    layers, _, parts, _ = w_proj.shape
    vmem = pl.BlockSpec(memory_space=pltpu.VMEM)
    hbm = pl.BlockSpec(memory_space=pl.ANY)
    dma = pltpu.SemaphoreType.DMA
    out = pl.pallas_call(
        functools.partial(window_kernel, rows, chs),
        out_shape=pltpu.VMEM((n, block), BF16),
        in_specs=[hbm] * 11,
        out_specs=vmem,
        scratch_shapes=[
            pltpu.SMEM(residue_mask.shape, jnp.int32),
            pltpu.SMEM(chain_ids.shape, jnp.int32),
            pltpu.VMEM((2, layers, lanes), F32),
            pltpu.VMEM((n, block), BF16),
            pltpu.VMEM((rows * chs, n, block), BF16),
            pltpu.VMEM((chs, (2 * parts + 3) * block, lanes), BF16),
            pltpu.VMEM((block, lanes), BF16),
            pltpu.VMEM((chs, 3, layers, block), F32),
            pltpu.VMEM((n * n, lanes), F32),
            pltpu.VMEM((n * n, lanes), F32),
            pltpu.VMEM((n * n, lanes), F32),
            pltpu.SemaphoreType.REGULAR,
            pltpu.SemaphoreType.REGULAR,
            dma((2,)),
            dma,
            dma,
            dma,
            dma,
            dma,
            dma,
            dma((3,)),
            dma((chs // 2 - 1, 3)),
            dma,
        ],
        compiler_params=pltpu.CompilerParams(collective_id=0, has_side_effects=True),
    )(
        residue_mask,
        chain_ids,
        jnp.swapaxes(pair_rep[:, 0, :], 0, 1),
        in_gain,
        in_bias,
        jnp.transpose(w_proj, (0, 2, 3, 1)).reshape(layers, parts * block, lanes),
        jnp.swapaxes(w_gate, 1, 2),
        pair_bias,
        out_gain,
        out_bias,
        w_out,
    )
    return jnp.swapaxes(out, 0, 1)[:, None, :]


def channel_norm(values, norm_gain, norm_bias):
    mean_val = jnp.mean(values, axis=0)
    variance = jnp.mean(values * values, axis=0) - mean_val * mean_val
    return (values - mean_val) * lax.rsqrt(variance + epsilon) * norm_gain[
        :, None, None
    ] + norm_bias[:, None, None]


def prepare(
    pair_local, layer, in_gain, in_bias, w_proj, w_gate, pair_bias, mask_rows, mask_cols, same_chain
):
    full_pair = lax.all_gather(pair_local, "ch", axis=0, tiled=True)
    normed = channel_norm(full_pair.astype(jnp.float32), in_gain[layer], in_bias[layer]).astype(
        jnp.bfloat16
    )
    projected = jnp.einsum(
        "cij,cpd->pdij", normed, w_proj[layer], preferred_element_type=jnp.float32
    )
    pair_mask = mask_rows[:, None] * mask_cols[None, :]
    first_arm = (jax.nn.sigmoid(projected[0]) * projected[1] * pair_mask).astype(jnp.bfloat16)
    second_arm = (jax.nn.sigmoid(projected[2]) * projected[3] * pair_mask).astype(jnp.bfloat16)
    logits = jnp.einsum("cij,cd->dij", normed, w_gate[layer], preferred_element_type=jnp.float32)
    logits = logits + pair_bias[layer][:, None, None] * same_chain[None]
    return (first_arm, second_arm, jax.nn.sigmoid(logits))


def finish(product_sum, gating, layer, out_gain, out_bias, w_out):
    totals = lax.psum(
        (jnp.sum(product_sum, axis=0), jnp.sum(product_sum * product_sum, axis=0)), "ch"
    )
    channels = product_sum.shape[0] * lax.axis_size("ch")
    mean_val = totals[0] / channels
    variance = totals[1] / channels - mean_val * mean_val
    scaled = (product_sum - mean_val) * lax.rsqrt(variance + epsilon)
    normed = (scaled * out_gain[layer][:, None, None] + out_bias[layer][:, None, None]).astype(
        jnp.bfloat16
    )
    columns = w_out[layer]
    mixed = lax.psum_scatter(
        jnp.einsum("dij,dc->cij", normed, columns, preferred_element_type=jnp.float32).astype(
            jnp.bfloat16
        ),
        "ch",
        scatter_dimension=0,
        tiled=True,
    ).astype(jnp.float32)
    return gating * mixed


def body(
    pair_rep,
    residue_mask,
    chain_ids,
    in_gain,
    in_bias,
    w_proj,
    w_gate,
    pair_bias,
    out_gain,
    out_bias,
    w_out,
):
    rows_here = pair_rep.shape[1]
    row_start = lax.axis_index("row") * rows_here
    mask_cols = residue_mask.astype(jnp.float32)
    mask_rows = lax.dynamic_slice_in_dim(mask_cols, row_start, rows_here)
    chain_rows = lax.dynamic_slice_in_dim(chain_ids, row_start, rows_here)
    same_chain = (chain_rows[:, None] == chain_ids[None, :]).astype(jnp.float32)
    first_arm, second_arm, gating = prepare(
        pair_rep, 0, in_gain, in_bias, w_proj, w_gate, pair_bias, mask_rows, mask_cols, same_chain
    )
    product_sum = jnp.einsum(
        "cik,cjk->cij",
        first_arm,
        lax.all_gather(second_arm, "row", axis=1, tiled=True),
        preferred_element_type=jnp.float32,
    )
    middle = (
        pair_rep.astype(jnp.float32) + finish(product_sum, gating, 0, out_gain, out_bias, w_out)
    ).astype(jnp.bfloat16)
    in_first, in_second, in_gating = prepare(
        middle, 1, in_gain, in_bias, w_proj, w_gate, pair_bias, mask_rows, mask_cols, same_chain
    )
    exchanged_left = lax.all_to_all(in_first, "row", split_axis=2, concat_axis=1, tiled=True)
    left_rows = jnp.swapaxes(exchanged_left, 1, 2)
    in_product = jnp.einsum(
        "cik,ckj->cij",
        left_rows,
        lax.all_gather(in_second, "row", axis=1, tiled=True),
        preferred_element_type=jnp.float32,
    )
    update = finish(in_product, in_gating, 1, out_gain, out_bias, w_out)
    return (middle.astype(jnp.float32) + update).astype(jnp.bfloat16)


def choose(rows, chs, *args):
    pair_rep, in_gain = args[0], args[3]
    n, lanes = pair_rep.shape[2], in_gain.shape[1]
    one_tile = pair_rep.shape[1] == 1 and n == rows == 8 and lanes == 128
    if one_tile and chs > 2 and chs % 2 == 0 and args[5].shape[1] == pair_rep.shape[0] * chs:
        return window_body(rows, chs, *args)
    return body(*args)


def solution(mesh):
    return jax.shard_map(
        functools.partial(choose, mesh.shape["row"], mesh.shape["ch"]),
        mesh=mesh,
        in_specs=(
            P("ch", "row", None),
            P(),
            P(),
            P(),
            P(),
            P(None, None, None, "ch"),
            P(None, None, "ch"),
            P(None, "ch"),
            P(None, "ch"),
            P(None, "ch"),
            P(None, "ch", None),
        ),
        out_specs=P("ch", "row", None),
        check_vma=False,
    )
```

```python
import functools
import jax
import jax.numpy as jnp
from jax import lax
from jax.experimental import pallas as pl
from jax.experimental.pallas import tpu as pltpu
from jax.sharding import PartitionSpec as P

epsilon = 1e-05
MESH = pl.DeviceIdType.MESH
F32 = jnp.float32
BF16 = jnp.bfloat16


def lane_norm(values, gain, bias):
    mean_val = jnp.mean(values, axis=-1, keepdims=True)
    variance = jnp.mean(values * values, axis=-1, keepdims=True) - mean_val * mean_val
    return ((values - mean_val) * lax.rsqrt(variance + epsilon) * gain + bias).astype(BF16)


def dot_nt(a, b):
    return lax.dot_general(a, b, (((1,), (1,)), ((), ())), preferred_element_type=F32)


def dot_nn(a, b):
    return lax.dot_general(a, b, (((1,), (0,)), ((), ())), preferred_element_type=F32)


def drain(ref, sem):
    pltpu.make_async_copy(ref, ref, sem).wait()


def window_kernel(
    rows,
    chs,
    mask_hbm,
    chain_hbm,
    pair_hbm,
    in_gain_hbm,
    in_bias_hbm,
    proj_hbm,
    gate_hbm,
    bias_hbm,
    gain_hbm,
    offset_hbm,
    mix_hbm,
    out_ref,
    mask_ref,
    chain_ref,
    norm_buf,
    own_buf,
    block_buf,
    weight_buf,
    last_gate_buf,
    vector_buf,
    left_buf,
    right_buf,
    middle_buf,
    near_sem,
    ready_sem,
    scalar_sem,
    norm_sem,
    own_sem,
    block_send,
    block_recv,
    vector_send,
    weight_send,
    parcel_recv,
    far_recv,
    gate_sem,
):
    n = out_ref.shape[0]
    lanes = norm_buf.shape[2]
    block = lanes // chs
    depth = proj_hbm.shape[1]
    split = depth + 2 * block
    row = lax.axis_index("row")
    ch = lax.axis_index("ch")
    here = row * chs + ch

    last = rows - 1
    cores = 2
    partner = ch + 1 - 2 * lax.rem(ch, cores)
    far = [lax.rem(ch + cores * step, chs) for step in range(1, chs // cores)]
    mates = far + [partner]
    is_last = here == rows * chs - 1

    barrier = pltpu.get_barrier_semaphore()

    def greet(r, c):
        pl.semaphore_signal(barrier, inc=1, device_id=(r, c), device_id_type=MESH)

    @pl.when(jnp.logical_not(is_last))
    def _():
        greet(last, chs - 1)

    @pl.when(here < cores)
    def _():
        for m in reversed(range(chs - 1)):
            greet(last, m)

        @pl.loop(1, last)
        def _(back):
            for m in range(chs):
                greet(last - back, m)

        @pl.loop(ch + 1, chs)
        def _(other):
            greet(0, other)

    lower_mates = lax.rem(ch, cores) + ch // cores
    greeted_above = jnp.minimum(ch, cores) + jnp.where(ch < cores, 0, lower_mates - 1)
    greetings = jnp.where(
        row == 0,
        greeted_above,
        jnp.where(row < last, cores + lower_mates, jnp.where(is_last, rows * chs - 1, cores)),
    )

    def send(src, dst, send_sem, recv_sem, r, c):
        pltpu.make_async_remote_copy(
            src_ref=src,
            dst_ref=dst,
            send_sem=send_sem,
            recv_sem=recv_sem,
            device_id=(r, c),
            device_id_type=MESH,
        ).start()

    def send_block(src, r, c):
        send(src, block_buf.at[ch * rows + row], block_send, block_recv, r, c)

    @pl.when(here > 0)
    def _():
        pl.semaphore_wait(barrier, greetings)

    for m in range(cores):

        @pl.when(here > m)
        def _():
            send_block(pair_hbm, 0, m)

    for mate in mates:

        @pl.when((mate > ch) & (row < last) & (here >= cores))
        def _():
            greet(row, mate)

    @pl.when(is_last)
    def _():
        @pl.loop(0, last)
        def _(other):
            for m in range(chs):
                pl.semaphore_signal(ready_sem, inc=1, device_id=(other, m), device_id_type=MESH)

        for m in range(chs - 1):
            pl.semaphore_signal(ready_sem, inc=1, device_id=(last, m), device_id_type=MESH)

    for mate in mates:

        @pl.when((mate < ch) & (row < last))
        def _():
            pl.semaphore_signal(near_sem, inc=1, device_id=(row, mate), device_id_type=MESH)

    pltpu.make_async_copy(pair_hbm, own_buf, own_sem).start()
    pltpu.make_async_copy(pair_hbm, block_buf.at[ch * rows + row], block_recv).start()
    vectors = [
        (ref, vector_buf.at[ch, t], vector_send, 2)
        for t, ref in enumerate((bias_hbm, gain_hbm, offset_hbm))
    ]
    pieces = (
        (0, proj_hbm, weight_buf, 0, depth),
        (0, gate_hbm, weight_buf, depth, block),
        (0, mix_hbm, weight_buf, depth + block, block),
        (1, proj_hbm, weight_buf, split, depth),
        (1, mix_hbm, weight_buf, split + depth, block),
    )
    weights = [
        (ref.at[u], buf.at[ch, pl.ds(at, size)], weight_send, u)
        for u, ref, buf, at, size in pieces
    ]
    parcels = weights[:3] + vectors + weights[3:]
    for src, dst, _, k in parcels:
        pltpu.make_async_copy(src, dst, parcel_recv.at[k]).start()
    pltpu.make_async_copy(mask_hbm, mask_ref, scalar_sem.at[0]).start()
    pltpu.make_async_copy(chain_hbm, chain_ref, scalar_sem.at[1]).start()
    pltpu.make_async_copy(in_gain_hbm, norm_buf.at[0], norm_sem).start()
    pltpu.make_async_copy(in_bias_hbm, norm_buf.at[1], norm_sem).start()
    pltpu.make_async_copy(gate_hbm.at[1], last_gate_buf, gate_sem).start()

    def give(step):
        for src, dst, send_sem, k in parcels:
            recv_sem = far_recv.at[step, k] if step < len(far) else parcel_recv.at[k]
            send(src, dst, send_sem, recv_sem, row, mates[step])

    for step, mate in enumerate(mates):

        @pl.when((mate < ch) & (row < last))
        def _():
            give(step)

    @pl.when((row < last) & (ch < chs - 1))
    def _():
        pl.semaphore_wait(near_sem, len(mates) - lower_mates)

    @pl.when((row == last) & jnp.logical_not(is_last))
    def _():
        pl.semaphore_wait(ready_sem, 1)

    for step, mate in enumerate(mates):

        @pl.when((mate > ch) | (row == last))
        def _():
            give(step)

    def pass_on():
        for k, buf, send_sem in (
            (0, weight_buf.at[:, pl.ds(0, split)], weight_send),
            (2, vector_buf, vector_send),
            (1, weight_buf.at[:, pl.ds(split, depth + block)], weight_send),
        ):
            for step in range(len(far)):
                piece = buf.at[lax.rem(ch + chs - cores * (step + 1), chs)]
                drain(piece, far_recv.at[step, k])
                send(piece, piece, send_sem, parcel_recv.at[k], row, partner)

    drain(own_buf, own_sem)

    @pl.when(here < cores)
    def _():
        pass_on()

    @pl.when(row < last)
    def _():
        pl.semaphore_wait(ready_sem, 1)

    for m in reversed(range(1, chs)):

        @pl.when(here < m if m < cores else (here != m))
        def _():
            send_block(own_buf, 0, m)

    @pl.when(row > 0)
    def _():
        for step in range(1, chs):
            send_block(own_buf, row, lax.rem(ch + step, chs))

    @pl.loop(1, row)
    def _(other):
        for m in reversed(range(chs)):
            send_block(own_buf, other, m)

    @pl.loop(row + 1, rows)
    def _(other):
        for m in reversed(range(chs)):
            send_block(own_buf, other, m)

    @pl.when(here >= cores)
    def _():
        pass_on()

    drain(mask_hbm, scalar_sem.at[0])
    drain(chain_hbm, scalar_sem.at[1])
    place = lax.broadcasted_iota(jnp.int32, (n, lanes), 0)
    mask_j = jnp.zeros((n, lanes), jnp.int32)
    chain_j = jnp.zeros((n, lanes), jnp.int32)
    for j in range(n):
        mask_j = jnp.where(place == j, mask_ref[j], mask_j)
        chain_j = jnp.where(place == j, chain_ref[j], chain_j)
    pair_mask = jnp.concatenate([(mask_j * mask_ref[i]).astype(F32) for i in range(n)], axis=0)
    same_chain = jnp.concatenate(
        [jnp.where(chain_j == chain_ref[i], 1.0, 0.0).astype(F32) for i in range(n)], axis=0
    )
    same_here = jnp.where(chain_j == chain_ref[row], 1.0, 0.0).astype(F32)

    def vector(t, u):
        return jnp.concatenate([vector_buf[m, t, u : u + 1, :] for m in range(chs)], axis=1)

    drain(norm_buf, norm_sem)
    drain(vector_buf.at[pl.ds(0, chs - len(far))], parcel_recv.at[2])
    bias = (0.5 * vector(0, 0)) * same_chain
    gains = [vector(1, u) for u in range(2)]
    offsets = [vector(2, u) for u in range(2)]
    last_bias = (0.5 * vector_buf[ch, 0, 1:2, :]) * same_here[:, 0:block]

    picked = lax.broadcasted_iota(jnp.int32, (block, lanes), 1)
    wanted = lax.broadcasted_iota(jnp.int32, (block, lanes), 0) + ch * block
    chosen = jnp.where(picked == wanted, 1.0, 0.0).astype(BF16)
    diagonal = lax.broadcasted_iota(jnp.int32, (lanes, lanes), 0) == lax.broadcasted_iota(
        jnp.int32, (lanes, lanes), 1
    )
    def halves(values):
        high = values.astype(BF16)
        return high, (values - high.astype(F32)).astype(BF16)

    def tail_of(*rows_of):
        count = 2 * n
        place_of = lax.broadcasted_iota(jnp.int32, (count, rows_of[0].shape[1]), 0)
        tail = jnp.zeros(place_of.shape, F32)
        for i, values in enumerate(rows_of):
            tail = jnp.where(place_of == i, values.astype(F32), tail)
        return tail.astype(BF16)

    one = jnp.ones((1, lanes), F32)
    in_tails, out_tails = [], []
    for u in range(2):
        ratio = norm_buf[1, u : u + 1, :] / norm_buf[0, u : u + 1, :]
        in_tails.append(tail_of(one, *halves(ratio)))
        out_tails.append(tail_of(one, *halves(offsets[u] / gains[u])))

    def statistics(values):
        mean_val = jnp.mean(values, axis=-1, keepdims=True)
        variance = jnp.mean(values * values, axis=-1, keepdims=True) - mean_val * mean_val
        scale = lax.rsqrt(variance + epsilon)
        return scale, scale * mean_val

    def gate_of(values):
        return jnp.tanh(values) + 1.0

    def fold(dot, scaled, tail):
        product = dot(tail, scaled)
        return scaled, product[0:1], product[1:2] + product[2:3]

    def normed_product(product, stats, folded):
        return product * stats[0] + (folded[2] - stats[1] * folded[1])

    def fold_in(u, weight):
        scaled = (weight.astype(F32) * (0.5 * norm_buf[0, u : u + 1, :])).astype(BF16)
        return fold(dot_nt, scaled, in_tails[u])

    def fold_out(u, weight):
        column = jnp.sum(jnp.where(diagonal, gains[u], 0.0), axis=-1, keepdims=True)
        scaled = (weight.astype(F32) * (0.5 * column)).astype(BF16)
        return fold(dot_nn, scaled, out_tails[u])

    def parts_of(u, buf, at):
        weights = [
            buf[:, at + part * block : at + (part + 1) * block, :].reshape(lanes, lanes)
            for part in range(depth // block)
        ]
        return [
            fold_in(u, jnp.concatenate(weights[first : first + 4], axis=0))
            for first in range(0, len(weights), 4)
        ]

    def arms(values, stats, folded):
        value = [normed_product(dot_nt(values, part[0]), stats, part) for part in folded]
        value = [
            wide[:, first : first + lanes]
            for wide in value
            for first in range(0, wide.shape[1], lanes)
        ]
        left_buf[...] = gate_of(value[0]) * (value[1] * pair_mask)
        right_buf[...] = gate_of(value[2]) * (value[3] * pair_mask)

    def mix(values, folded):
        both = jnp.concatenate(halves(values), axis=1)
        product = dot_nn(both, jnp.concatenate([folded[0], folded[0]], axis=0))
        return normed_product(product, statistics(values), folded)

    drain(last_gate_buf, gate_sem)
    drain(weight_buf.at[pl.ds(0, chs - len(far)), pl.ds(0, split)], parcel_recv.at[0])
    first_parts = parts_of(0, weight_buf, 0)
    first_gate = fold_in(0, weight_buf[:, depth : depth + block, :].reshape(lanes, lanes))
    first_mix = fold_out(0, weight_buf[:, depth + block : split, :].reshape(lanes, lanes))
    drain(weight_buf.at[pl.ds(0, chs - len(far)), pl.ds(split, depth + block)], parcel_recv.at[1])
    second_parts = parts_of(1, weight_buf, split)
    last_gate = fold_in(1, last_gate_buf[...])
    last_mix = fold_out(
        1, dot_nt(weight_buf[:, split + depth :, :].reshape(lanes, lanes), chosen).astype(BF16)
    )

    drain(block_buf, block_recv)
    values = jnp.concatenate(
        [block_buf[m * rows : (m + 1) * rows].reshape(n * n, block) for m in range(chs)], axis=1
    )
    pair = values.astype(F32)
    stats = statistics(pair)
    arms(values, stats, first_parts)
    gating = gate_of(normed_product(dot_nt(values, first_gate[0]), stats, first_gate) + bias)
    right_k = [right_buf[pl.ds(k, n, stride=n), :] for k in range(n)]
    product = []
    for i in range(n):
        total = left_buf[i * n : i * n + 1, :] * right_k[0]
        for k in range(1, n):
            total = total + left_buf[i * n + k : i * n + k + 1, :] * right_k[k]
        product.append(total)
    mixed = mix(jnp.concatenate(product, axis=0), first_mix)
    values = (pair + gating * mixed).astype(BF16)
    middle = values.astype(F32)
    middle_buf[...] = middle

    arms(values, statistics(middle), second_parts)
    mine = middle_buf[pl.ds(pl.multiple_of(row * n, n), n), :]
    logits = normed_product(dot_nt(mine.astype(BF16), last_gate[0]), statistics(mine), last_gate)
    gating = gate_of(logits + last_bias)
    kept = dot_nt(mine.astype(BF16), chosen)
    total = left_buf[pl.ds(row, 1), :] * right_buf[0:n, :]
    for k in range(1, n):
        total = total + left_buf[pl.ds(k * n + row, 1), :] * right_buf[k * n : (k + 1) * n, :]
    out_ref[...] = (kept + gating * mix(total, last_mix)).astype(BF16)

    drain(block_buf.at[pl.ds(0, rows * chs - 1)], block_send)
    drain(vector_buf.at[pl.ds(0, chs - 1)], vector_send)
    drain(weight_buf.at[pl.ds(0, chs - 1)], weight_send)


def window_body(
    rows,
    chs,
    pair_rep,
    residue_mask,
    chain_ids,
    in_gain,
    in_bias,
    w_proj,
    w_gate,
    pair_bias,
    out_gain,
    out_bias,
    w_out,
):
    block, _, n = pair_rep.shape
    lanes = in_gain.shape[1]
    layers, _, parts, _ = w_proj.shape
    vmem = pl.BlockSpec(memory_space=pltpu.VMEM)
    hbm = pl.BlockSpec(memory_space=pl.ANY)
    dma = pltpu.SemaphoreType.DMA
    out = pl.pallas_call(
        functools.partial(window_kernel, rows, chs),
        out_shape=pltpu.VMEM((n, block), BF16),
        in_specs=[hbm] * 11,
        out_specs=vmem,
        scratch_shapes=[
            pltpu.SMEM(residue_mask.shape, jnp.int32),
            pltpu.SMEM(chain_ids.shape, jnp.int32),
            pltpu.VMEM((2, layers, lanes), F32),
            pltpu.VMEM((n, block), BF16),
            pltpu.VMEM((rows * chs, n, block), BF16),
            pltpu.VMEM((chs, (2 * parts + 3) * block, lanes), BF16),
            pltpu.VMEM((block, lanes), BF16),
            pltpu.VMEM((chs, 3, layers, block), F32),
            pltpu.VMEM((n * n, lanes), F32),
            pltpu.VMEM((n * n, lanes), F32),
            pltpu.VMEM((n * n, lanes), F32),
            pltpu.SemaphoreType.REGULAR,
            pltpu.SemaphoreType.REGULAR,
            dma((2,)),
            dma,
            dma,
            dma,
            dma,
            dma,
            dma,
            dma((3,)),
            dma((chs // 2 - 1, 3)),
            dma,
        ],
        compiler_params=pltpu.CompilerParams(collective_id=0, has_side_effects=True),
    )(
        residue_mask,
        chain_ids,
        jnp.swapaxes(pair_rep[:, 0, :], 0, 1),
        in_gain,
        in_bias,
        jnp.transpose(w_proj, (0, 2, 3, 1)).reshape(layers, parts * block, lanes),
        jnp.swapaxes(w_gate, 1, 2),
        pair_bias,
        out_gain,
        out_bias,
        w_out,
    )
    return jnp.swapaxes(out, 0, 1)[:, None, :]


def channel_norm(values, norm_gain, norm_bias):
    mean_val = jnp.mean(values, axis=0)
    variance = jnp.mean(values * values, axis=0) - mean_val * mean_val
    return (values - mean_val) * lax.rsqrt(variance + epsilon) * norm_gain[
        :, None, None
    ] + norm_bias[:, None, None]


def prepare(
    pair_local, layer, in_gain, in_bias, w_proj, w_gate, pair_bias, mask_rows, mask_cols, same_chain
):
    full_pair = lax.all_gather(pair_local, "ch", axis=0, tiled=True)
    normed = channel_norm(full_pair.astype(jnp.float32), in_gain[layer], in_bias[layer]).astype(
        jnp.bfloat16
    )
    projected = jnp.einsum(
        "cij,cpd->pdij", normed, w_proj[layer], preferred_element_type=jnp.float32
    )
    pair_mask = mask_rows[:, None] * mask_cols[None, :]
    first_arm = (jax.nn.sigmoid(projected[0]) * projected[1] * pair_mask).astype(jnp.bfloat16)
    second_arm = (jax.nn.sigmoid(projected[2]) * projected[3] * pair_mask).astype(jnp.bfloat16)
    logits = jnp.einsum("cij,cd->dij", normed, w_gate[layer], preferred_element_type=jnp.float32)
    logits = logits + pair_bias[layer][:, None, None] * same_chain[None]
    return (first_arm, second_arm, jax.nn.sigmoid(logits))


def finish(product_sum, gating, layer, out_gain, out_bias, w_out):
    totals = lax.psum(
        (jnp.sum(product_sum, axis=0), jnp.sum(product_sum * product_sum, axis=0)), "ch"
    )
    channels = product_sum.shape[0] * lax.axis_size("ch")
    mean_val = totals[0] / channels
    variance = totals[1] / channels - mean_val * mean_val
    scaled = (product_sum - mean_val) * lax.rsqrt(variance + epsilon)
    normed = (scaled * out_gain[layer][:, None, None] + out_bias[layer][:, None, None]).astype(
        jnp.bfloat16
    )
    columns = w_out[layer]
    mixed = lax.psum_scatter(
        jnp.einsum("dij,dc->cij", normed, columns, preferred_element_type=jnp.float32).astype(
            jnp.bfloat16
        ),
        "ch",
        scatter_dimension=0,
        tiled=True,
    ).astype(jnp.float32)
    return gating * mixed


def body(
    pair_rep,
    residue_mask,
    chain_ids,
    in_gain,
    in_bias,
    w_proj,
    w_gate,
    pair_bias,
    out_gain,
    out_bias,
    w_out,
):
    rows_here = pair_rep.shape[1]
    row_start = lax.axis_index("row") * rows_here
    mask_cols = residue_mask.astype(jnp.float32)
    mask_rows = lax.dynamic_slice_in_dim(mask_cols, row_start, rows_here)
    chain_rows = lax.dynamic_slice_in_dim(chain_ids, row_start, rows_here)
    same_chain = (chain_rows[:, None] == chain_ids[None, :]).astype(jnp.float32)
    first_arm, second_arm, gating = prepare(
        pair_rep, 0, in_gain, in_bias, w_proj, w_gate, pair_bias, mask_rows, mask_cols, same_chain
    )
    product_sum = jnp.einsum(
        "cik,cjk->cij",
        first_arm,
        lax.all_gather(second_arm, "row", axis=1, tiled=True),
        preferred_element_type=jnp.float32,
    )
    middle = (
        pair_rep.astype(jnp.float32) + finish(product_sum, gating, 0, out_gain, out_bias, w_out)
    ).astype(jnp.bfloat16)
    in_first, in_second, in_gating = prepare(
        middle, 1, in_gain, in_bias, w_proj, w_gate, pair_bias, mask_rows, mask_cols, same_chain
    )
    exchanged_left = lax.all_to_all(in_first, "row", split_axis=2, concat_axis=1, tiled=True)
    left_rows = jnp.swapaxes(exchanged_left, 1, 2)
    in_product = jnp.einsum(
        "cik,ckj->cij",
        left_rows,
        lax.all_gather(in_second, "row", axis=1, tiled=True),
        preferred_element_type=jnp.float32,
    )
    update = finish(in_product, in_gating, 1, out_gain, out_bias, w_out)
    return (middle.astype(jnp.float32) + update).astype(jnp.bfloat16)


def choose(rows, chs, *args):
    pair_rep, in_gain = args[0], args[3]
    n, lanes = pair_rep.shape[2], in_gain.shape[1]
    one_tile = pair_rep.shape[1] == 1 and n == rows == 8 and lanes == 128
    if one_tile and chs > 2 and chs % 2 == 0 and args[5].shape[1] == pair_rep.shape[0] * chs:
        return window_body(rows, chs, *args)
    return body(*args)


def solution(mesh):
    return jax.shard_map(
        functools.partial(choose, mesh.shape["row"], mesh.shape["ch"]),
        mesh=mesh,
        in_specs=(
            P("ch", "row", None),
            P(),
            P(),
            P(),
            P(),
            P(None, None, None, "ch"),
            P(None, None, "ch"),
            P(None, "ch"),
            P(None, "ch"),
            P(None, "ch"),
            P(None, "ch", None),
        ),
        out_specs=P("ch", "row", None),
        check_vma=False,
    )
```
